32 devices in a mesh: var: 8 (over y, x, core), head: 4 (over z).
Axes of the slice: x: 2, y: 2, z: 4, core: 2. Of those that a mesh axis runs over, the one named last changes fastest.
Arguments:
- series: float32 [1024, 8192], P('var', 'head'), may hold values from -48 to 48
- emb_weight: float32 [8192, 512], P('head'), as said below
- emb_bias: float32 [512], replicated, may hold values from -3 to 3
- q_weight: float32 [512, 512], P(None, 'head'), may hold values from -0.75 to 0.75
- k_weight: float32 [512, 512], P(None, 'head'), may hold values from -0.25 to 0.25
- v_weight: float32 [512, 512], P(None, 'head'), may hold values from -0.25 to 0.25
- out_weight: float32 [512, 512], P('head'), may hold values from -0.25 to 0.25
- norm1_gain: float32 [512], replicated, may hold values from 0.1 to 1.9
- norm1_bias: float32 [512], replicated, may hold values from -3 to 3
- ffn_in: float32 [512, 2048], P(None, 'head'), may hold values from -0.25 to 0.25
- ffn_out: float32 [2048, 512], P('head'), may hold values from -0.1875 to 0.1875
- norm2_gain: float32 [512], replicated, may hold values from 0.1 to 1.9
- norm2_bias: float32 [512], replicated, may hold values from -3 to 3
Outputs:
- final: float32 [512, 1024], P('head', 'var')
The draws below stay inside these ranges and needn't reach their ends.
Inputs may be any that keep to these rules, and one draw needn't show every extreme that they name: `emb_weight`: every entry lies within 12 / sqrt(8192) in magnitude, and some entry reaches that bound.
All inputs are finite; a program needn't handle non-finite values.
Results may differ from the reference program's by a relative error of at most 0.0003.
Values sent between devices are 32-bit elements; how exact they have to be, the bound alone decides.
No kernel may reach another device: no remote copies, remote signals or barrier semaphores. Data moves between devices by JAX's collectives and lax.ppermute only.
A program may use at most 64 MiB of HBM per device.

```python
import math
import jax
import jax.numpy as jnp
from jax import lax

D = 512
FF = 2048
H = 8
L = 8192
DH = 64
VARS = 1024


def draw_series(key, part):
    base = jnp.clip(jax.random.normal(jax.random.fold_in(key, 11), (VARS, L), jnp.float32), -6.0, 6.0)
    base = base.at[0, 0].set(6.0)
    return base


def draw_emb_weight(key, part):
    base = jnp.clip(jax.random.normal(jax.random.fold_in(key, 21), (L, D), jnp.float32), -4.0, 4.0)
    base = base.at[0, D - 1].set(4.0)
    column_scale = jnp.exp(jnp.linspace(math.log(0.4), math.log(3.0), D, dtype=jnp.float32))
    return base * column_scale[None, :] / math.sqrt(L)


def with_spikes(values, own_key, source, target, parts, factor):
    def block_of(axis_at):
        return (jnp.arange(values.shape[axis_at]) // (values.shape[axis_at] // parts)).reshape((-1,) + (1,) * (values.ndim - 1 - axis_at))

    one_side = jax.random.permutation(own_key, parts)[block_of(target)]
    far = (block_of(target) + parts // 2) % parts
    return jnp.where((block_of(source) == one_side) | (block_of(source) == far), factor * values, values)


def level_of(stream_key, dims, cuts, smallest, high):
    factor_of = 1.0
    for axis_at, shards_of in cuts:
        steps = jax.random.uniform(jax.random.fold_in(jax.random.fold_in(stream_key, 6), axis_at), (shards_of,), jnp.float32, smallest / len(cuts), high / len(cuts))
        factor_of = factor_of * jnp.repeat(jnp.exp(steps), dims[axis_at] // shards_of).reshape((-1,) + (1,) * (len(dims) - 1 - axis_at))
    return factor_of


def bell_draw(own_key, shape, scale, bound, pieces=(), held_as=jnp.bfloat16):
    values = scale * jax.random.normal(own_key, shape, jnp.float32)
    if pieces:
        values = values * level_of(own_key, shape, pieces, -0.22, 0.18)
    return jnp.clip(values, -bound, bound).astype(held_as)


def gaussian_with(rng, shape, scale, reach, cuts, heavy, kind=jnp.bfloat16):
    drawn = scale * jax.random.normal(rng, shape, jnp.float32)
    if cuts:
        drawn = drawn * level_of(rng, shape, cuts, -0.22, 0.18)
    return jnp.clip(with_spikes(drawn, jax.random.fold_in(rng, 3), *heavy), -reach, reach).astype(kind)


def setup_inputs(seed: int = 0) -> dict:
    streams_of = jax.random.split(jax.random.key(seed), 14)
    return {
        "series": draw_series(jax.random.fold_in(streams_of[13], 71), 0),
        "emb_weight": draw_emb_weight(jax.random.fold_in(streams_of[13], 71), 0),
        "emb_bias": bell_draw(streams_of[2], (D,), 0.5, 3.0, (), jnp.float32),
        "q_weight": bell_draw(streams_of[3], (D, D), (D // 9) ** -0.5, 0.75, ((1, 4),), jnp.float32),
        "k_weight": bell_draw(streams_of[4], (D, D), D ** -0.5, 0.25, ((1, 4),), jnp.float32),
        "v_weight": bell_draw(streams_of[5], (D, D), D ** -0.5, 0.25, ((1, 4),), jnp.float32),
        "out_weight": bell_draw(streams_of[6], (D, D), D ** -0.5, 0.25, ((0, 4),), jnp.float32),
        "norm1_gain": jnp.clip(1.0 + 0.18 * jax.random.normal(streams_of[7], (D,), jnp.float32), 0.1, 1.9),
        "norm1_bias": bell_draw(streams_of[8], (D,), 0.5, 3.0, (), jnp.float32),
        "ffn_in": bell_draw(streams_of[9], (D, FF), D ** -0.5, 0.25, ((1, 4),), jnp.float32),
        "ffn_out": gaussian_with(streams_of[10], (FF, D), FF ** -0.5, 0.1875, ((0, 4),), (0, 1, 4, 2.0), jnp.float32),
        "norm2_gain": jnp.clip(1.0 + 0.18 * jax.random.normal(streams_of[11], (D,), jnp.float32), 0.1, 1.9),
        "norm2_bias": bell_draw(streams_of[12], (D,), 0.5, 3.0, (), jnp.float32),
    }


HIGH = lax.Precision.HIGHEST

def product(first_op, second_op):
    return jnp.dot(first_op, second_op, precision=HIGH, preferred_element_type=jnp.float32)

def layer_norm(stream, scale_gain, shift_bias):
    centre = lax.optimization_barrier(jnp.mean(stream, axis=-1, keepdims=True))
    spread = stream - centre
    variance = lax.optimization_barrier(jnp.mean(spread * spread, axis=-1, keepdims=True))
    return spread * lax.rsqrt(variance + 1e-05) * scale_gain + shift_bias

def reference(series, emb_weight, emb_bias, q_weight, k_weight, v_weight, out_weight, norm1_gain, norm1_bias, ffn_in, ffn_out, norm2_gain, norm2_bias):
    embedded = product(series, emb_weight) + emb_bias
    queries = product(embedded, q_weight).reshape(VARS, H, DH).transpose(1, 0, 2)
    key_rows = product(embedded, k_weight).reshape(VARS, H, DH).transpose(1, 0, 2)
    values = product(embedded, v_weight).reshape(VARS, H, DH).transpose(1, 0, 2)
    block_len = math.gcd(VARS, 1024)
    score_scale = 1.0 / math.sqrt(DH)

    def one_head(operands):
        head_q, head_k, head_v = operands
        blocks = head_q.reshape(VARS // block_len, block_len, DH)

        def one_block(query_block):
            scores = lax.dot_general(query_block, head_k, (((1,), (1,)), ((), ())), precision=HIGH, preferred_element_type=jnp.float32) * score_scale
            row_max = lax.optimization_barrier(jnp.max(scores, axis=1, keepdims=True))
            weights = jnp.exp(scores - row_max)
            return product(weights, head_v) / lax.optimization_barrier(jnp.sum(weights, axis=1, keepdims=True))
        return lax.map(one_block, blocks).reshape(VARS, DH)
    mixed_rows = lax.map(one_head, (queries, key_rows, values))
    mixed_rows = mixed_rows.transpose(1, 0, 2).reshape(VARS, D)
    normed = layer_norm(embedded + product(mixed_rows, out_weight), norm1_gain, norm1_bias)
    hidden = jax.nn.gelu(product(normed, ffn_in), approximate=False)
    result_rows = layer_norm(normed + product(hidden, ffn_out), norm2_gain, norm2_bias)
    return result_rows.T
```

```python
import functools
import math

import jax
import jax.numpy as jnp
from jax import lax
from jax.experimental import pallas as pl
from jax.experimental.pallas import tpu as pltpu
from jax.sharding import PartitionSpec as P

DH = 64
EPS = 1e-05
F32 = jnp.float32
BF16 = jnp.bfloat16
MIB = 1 << 20


def split(x):
    hi = x.astype(BF16)
    return hi, (x - hi.astype(F32)).astype(BF16)


def mm(a, b, dims):
    return lax.dot_general(a, b, (dims, ((), ())), preferred_element_type=F32)


def dot3(a, b, dims=((1,), (0,))):
    a_hi, a_lo = split(a)
    b_hi, b_lo = split(b)
    rows = a.shape[0]
    first = mm(jnp.concatenate([a_hi, a_lo], 0), b_hi, dims)
    return first[:rows] + (first[rows:] + mm(a_hi, b_lo, dims))


def butterfly(blocks, pos):
    count = len(blocks)
    out = list(blocks)
    bit = 1
    while bit < count:
        take = (pos & bit) != 0
        out = [jnp.where(take, out[j ^ bit], out[j]) for j in range(count)]
        bit *= 2
    return out


def columns(x, count):
    width = x.shape[1] // count
    return [x[:, j * width : (j + 1) * width] for j in range(count)]


def call(body, outs, name, scratch=(), limit=12, grid=None, in_specs=None, out_specs=None, flops=0, nbytes=0):
    kwargs = {}
    if grid is not None:
        kwargs = dict(grid=grid, in_specs=in_specs, out_specs=out_specs)
    return pl.pallas_call(
        body,
        out_shape=outs,
        scratch_shapes=list(scratch),
        name=name,
        compiler_params=pltpu.CompilerParams(vmem_limit_bytes=limit * MIB),
        cost_estimate=pl.CostEstimate(flops=flops, bytes_accessed=nbytes, transcendentals=0),
        **kwargs,
    )


def shape(*dims):
    return jax.ShapeDtypeStruct(dims, F32)


def embed_kernel(count, x_ref, w_ref, *rest):
    outs, acc = rest[:count], rest[count]
    step = pl.program_id(0)
    pos = lax.axis_index("head")
    part = dot3(x_ref[...], w_ref[...])

    @pl.when(step == 0)
    def _():
        acc[...] = part

    @pl.when(step > 0)
    def _():
        acc[...] += part

    @pl.when(step == pl.num_programs(0) - 1)
    def _():
        for ref, block in zip(outs, butterfly(columns(acc[...], count), pos)):
            ref[...] = block


def embed_reduce_kernel(count, *refs):
    pos = lax.axis_index("head")
    parts, bias, out = refs[:count], refs[count], refs[count + 1]
    total = parts[0][...]
    for part in parts[1:]:
        total = total + part[...]
    out[...] = total + bias[pos]


def rows_of(weight, block, width):
    return weight[pl.ds(pl.multiple_of(block * width, width), width), :]


def project_kernel(count, scale, *refs):
    pos = lax.axis_index("head")
    blocks, weights, out = refs[:count], refs[count:-1], refs[-1]
    width = blocks[0].shape[1]
    stream = jnp.concatenate([block[...] for block in blocks], 1)
    at = 0
    for weight in weights:
        ordered = jnp.concatenate([rows_of(weight, pos ^ k, width) for k in range(count)], 0)
        result = dot3(stream, ordered)
        out[:, at : at + result.shape[1]] = result * scale if scale != 1.0 else result
        at += result.shape[1]


def attend_kernel(q_ref, *refs):
    pieces, out = refs[:-1], refs[-1]
    heads_width = q_ref.shape[1]
    for head in range(heads_width // DH):
        cols = slice(head * DH, (head + 1) * DH)
        vcols = slice(heads_width + head * DH, heads_width + (head + 1) * DH)
        query = q_ref[:, cols]
        keys = jnp.concatenate([piece[:, cols] for piece in pieces], 0)
        values = jnp.concatenate([piece[:, vcols] for piece in pieces], 0)
        scores = dot3(query, keys, ((1,), (1,)))
        top = jnp.max(scores, axis=1, keepdims=True)
        weights = jnp.exp(scores - top)
        total = jnp.sum(weights, axis=1, keepdims=True)
        out[:, cols] = dot3(weights, values) / total


def normalise(x, gain, bias):
    centre = jnp.mean(x, axis=-1, keepdims=True)
    spread = x - centre
    variance = jnp.mean(spread * spread, axis=-1, keepdims=True)
    return spread * lax.rsqrt(variance + EPS) * gain + bias


def gelu(v):
    return 0.5 * v * (1.0 + lax.erf(v * (1.0 / math.sqrt(2.0))))


def post_kernel(count, *refs):
    pos = lax.axis_index("head")
    mixed, owts, emb = refs[:count], refs[count : 2 * count], refs[2 * count : 3 * count]
    gain, bias, w_in, w_out = refs[3 * count : 3 * count + 4]
    outs = refs[3 * count + 4 :]
    stream = jnp.concatenate([m[...] for m in mixed], 1)
    weight = jnp.concatenate([w[...] for w in owts], 0)
    attention = dot3(stream, weight)
    embedded = jnp.concatenate(butterfly([e[...] for e in emb], pos), 1)
    normed = normalise(embedded + attention, gain[...], bias[...])
    hidden = gelu(dot3(normed, w_in[...]))
    partial = butterfly(columns(dot3(hidden, w_out[...]), count), pos)
    mine = butterfly(columns(normed, count), pos)[0]
    outs[0][...] = mine + partial[0]
    for ref, block in zip(outs[1:], partial[1:]):
        ref[...] = block


def stats_kernel(count, *refs):
    parts, out, stats = refs[:count], refs[count], refs[count + 1]
    total = parts[0][...]
    for part in parts[1:]:
        total = total + part[...]
    flipped = total.T
    centre = jnp.mean(flipped, axis=0, keepdims=True)
    spread = flipped - centre
    out[...] = flipped
    stats[...] = jnp.concatenate([centre, jnp.sum(spread * spread, axis=0, keepdims=True)], 0)


def final_kernel(count, x_ref, *refs):
    pos = lax.axis_index("head")
    stats, gain, bias, out = refs[:count], refs[count], refs[count + 1], refs[count + 2]
    width = x_ref.shape[0]
    centres = [s[0:1, :] for s in stats]
    centre = sum(centres[1:], centres[0]) * (1.0 / count)
    square = sum((s[1:2, :] for s in stats[1:]), stats[0][1:2, :])
    for each in centres:
        square = square + width * (each - centre) * (each - centre)
    scale = lax.rsqrt(square * (1.0 / (count * width)) + EPS)
    pair = jnp.concatenate([gain[pos], bias[pos], jnp.zeros((6, width), F32)], 0).T
    out[...] = (x_ref[...] - centre) * scale * pair[:, 0:1] + pair[:, 1:2]


def send(x, axis, offset):
    size = lax.axis_size(axis)
    return lax.ppermute(x, axis, [(i, i ^ offset) for i in range(size)])


def spread_out(x, axis):
    return [x] + [send(x, axis, k) for k in range(1, lax.axis_size(axis))]


def gather_pieces(piece):
    size = lax.axis_size("var")
    if size > 8:
        return [lax.all_gather(piece, "var", axis=0, tiled=True)]
    far = [piece] + [send(piece, "var", k) for k in range(2, size, 2)]
    return far + [send(each, "var", 1) for each in far]


def on_device(
    series, emb_weight, emb_bias, q_weight, k_weight, v_weight, out_weight,
    norm1_gain, norm1_bias, ffn_in, ffn_out, norm2_gain, norm2_bias,
):
    n = lax.axis_size("head")
    rows, depth = series.shape
    model = emb_weight.shape[1]
    width = model // n
    heads_width = q_weight.shape[1]
    block = shape(rows, width)

    chunk = math.gcd(depth, 512)
    parts = call(
        functools.partial(embed_kernel, n), [block] * n, "embed",
        scratch=[pltpu.VMEM((rows, model), F32)],
        grid=(depth // chunk,),
        in_specs=[
            pl.BlockSpec((rows, chunk), lambda i: (0, i)),
            pl.BlockSpec((chunk, model), lambda i: (i, 0)),
        ],
        out_specs=[pl.BlockSpec((rows, width), lambda i: (0, 0))] * n,
        flops=6 * rows * depth * model, nbytes=4 * depth * (rows + model),
    )(series, emb_weight)
    got = [parts[0]] + [send(parts[k], "head", k) for k in range(1, n)]
    mine = call(functools.partial(embed_reduce_kernel, n), block, "embed_sum")(
        *got, emb_bias.reshape(n, 1, width)
    )
    emb = spread_out(mine, "head")
    pair = call(functools.partial(project_kernel, n, 1.0), shape(rows, 2 * heads_width), "project_kv")(
        *emb, k_weight, v_weight
    )
    queries = call(
        functools.partial(project_kernel, n, 1.0 / math.sqrt(DH)), shape(rows, heads_width), "project_q"
    )(*emb, q_weight)
    pieces = gather_pieces(pair)
    late_weight, _ = lax.optimization_barrier((out_weight, pair))
    owts = spread_out(late_weight, "head")
    mixed = call(attend_kernel, shape(rows, heads_width), "attend", limit=16)(queries, *pieces)
    mixes = spread_out(mixed, "head")
    partial = call(functools.partial(post_kernel, n), [block] * n, "post", limit=16)(
        *mixes, *owts, *emb, norm1_gain[None, :], norm1_bias[None, :], ffn_in, ffn_out
    )
    got = [partial[0]] + [send(partial[k], "head", k) for k in range(1, n)]
    flipped, stats = call(
        functools.partial(stats_kernel, n), [shape(width, rows), shape(2, rows)], "stats"
    )(*got)
    return call(functools.partial(final_kernel, n), shape(width, rows), "final")(
        flipped, *spread_out(stats, "head"), norm2_gain.reshape(n, 1, width), norm2_bias.reshape(n, 1, width)
    )


def solution(mesh):
    return jax.shard_map(
        on_device,
        mesh=mesh,
        in_specs=(
            P("var", "head"), P("head", None), P(), P(None, "head"), P(None, "head"), P(None, "head"),
            P("head", None), P(), P(), P(None, "head"), P("head", None), P(), P(),
        ),
        out_specs=P("head", "var"),
        check_vma=False,
    )
```

```python
import functools
import math

import jax
import jax.numpy as jnp
from jax import lax
from jax.experimental import pallas as pl
from jax.experimental.pallas import tpu as pltpu
from jax.sharding import PartitionSpec as P


DH = 64
EPS = 1e-05
F32 = jnp.float32
BF16 = jnp.bfloat16
MIB = 1 << 20


def split(x):
    hi = x.astype(BF16)
    return hi, (x - hi.astype(F32)).astype(BF16)


def mm(a, b, dims):
    return lax.dot_general(a, b, (dims, ((), ())), preferred_element_type=F32)


def dot3(a, b, dims=((1,), (0,))):
    a_hi, a_lo = split(a)
    b_hi, b_lo = split(b)
    rows = a.shape[0]
    first = mm(jnp.concatenate([a_hi, a_lo], 0), b_hi, dims)
    return first[:rows] + (first[rows:] + mm(a_hi, b_lo, dims))


def butterfly(blocks, pos):
    count = len(blocks)
    out = list(blocks)
    bit = 1
    while bit < count:
        take = (pos & bit) != 0
        out = [jnp.where(take, out[j ^ bit], out[j]) for j in range(count)]
        bit *= 2
    return out


def columns(x, count):
    width = x.shape[1] // count
    return [x[:, j * width : (j + 1) * width] for j in range(count)]


def call(body, outs, scratch=(), limit=12, grid=None, in_specs=None, out_specs=None, flops=0, nbytes=0):
    kwargs = {}
    if grid is not None:
        kwargs = dict(grid=grid, in_specs=in_specs, out_specs=out_specs)
    return pl.pallas_call(
        body,
        out_shape=outs,
        scratch_shapes=list(scratch),
        compiler_params=pltpu.CompilerParams(vmem_limit_bytes=limit * MIB),
        cost_estimate=pl.CostEstimate(flops=flops, bytes_accessed=nbytes, transcendentals=0),
        **kwargs,
    )


def shape(*dims):
    return jax.ShapeDtypeStruct(dims, F32)


def embed_kernel(count, far, x_hbm, w_hbm, *rest):
    outs, (x_buf, w_buf, sems) = rest[: count // 2], rest[count // 2 :]
    pos = lax.axis_index("head")
    half = w_hbm.shape[1] // 2
    side = pos // (count // 2)
    side = 1 - side if far else side
    cols = pl.ds(pl.multiple_of(side * half, half), half)
    steps, step = w_buf.shape[0], w_buf.shape[1]
    copies = []
    for at in range(steps):
        span = pl.ds(at * step, step)
        copies.append(
            (
                pltpu.make_async_copy(x_hbm.at[:, span], x_buf.at[at], sems.at[0, at]),
                pltpu.make_async_copy(w_hbm.at[span, cols], w_buf.at[at], sems.at[1, at]),
            )
        )
        for copy in copies[-1]:
            copy.start()
    total = None
    for at in range(steps):
        for copy in copies[at]:
            copy.wait()
        part = dot3(x_buf[at], w_buf[at])
        total = part if total is None else total + part
    for ref, block in zip(outs, butterfly(columns(total, count // 2), pos)):
        ref[...] = block


def embed_half(count, far, series, emb_weight):
    rows, depth = series.shape
    half = emb_weight.shape[1] // 2
    step = math.gcd(depth, 256)
    steps = depth // step
    hbm = pl.BlockSpec(memory_space=pltpu.HBM)
    return pl.pallas_call(
        functools.partial(embed_kernel, count, far),
        out_shape=[shape(rows, 2 * half // count)] * (count // 2),
        in_specs=[hbm, hbm],
        scratch_shapes=[
            pltpu.VMEM((steps, rows, step), F32),
            pltpu.VMEM((steps, step, half), F32),
            pltpu.SemaphoreType.DMA((2, steps)),
        ],
        name="embed_far" if far else "embed_near",
        compiler_params=pltpu.CompilerParams(vmem_limit_bytes=(127 if far else 121) * MIB // 2),
        cost_estimate=pl.CostEstimate(flops=6 * rows * depth * half, bytes_accessed=4 * depth * half, transcendentals=0),
    )(series, emb_weight)


def piece_of(index, bits):
    return sum(((index >> bit) & 1) << at for at, bit in enumerate(bits))


def cut_kernel(bits, w_ref, out):
    part = piece_of(lax.axis_index("var"), bits)
    size = out.shape[0]
    out[...] = w_ref[pl.ds(pl.multiple_of(part * size, size), size), :]


def order_kernel(bits, own_ref, rest_ref, out):
    me = piece_of(lax.axis_index("var"), bits)
    rows = own_ref.shape[0]
    size = rows >> len(bits)
    out[0:rows, :] = own_ref[...]
    for apart in range(1 << len(bits)):
        for k in range(rest_ref.shape[1]):
            start = pl.multiple_of((k + 1) * rows + (me ^ apart) * size, size)
            out[pl.ds(start, size), :] = rest_ref[apart, k]


def embed_reduce_kernel(count, *refs):
    pos = lax.axis_index("head")
    parts, bias, out = refs[:count], refs[count], refs[count + 1]
    total = parts[0][...]
    for part in parts[1:]:
        total = total + part[...]
    out[...] = total + bias[pos]


def rows_of(weight, block, width):
    return weight[pl.ds(pl.multiple_of(block * width, width), width), :]


def project_kernel(count, scale, *refs):
    pos = lax.axis_index("head")
    blocks, weights, out = refs[:count], refs[count:-1], refs[-1]
    width = blocks[0].shape[1]
    stream = jnp.concatenate([block[...] for block in blocks], 1)
    at = 0
    for weight in weights:
        ordered = jnp.concatenate([rows_of(weight, pos ^ k, width) for k in range(count)], 0)
        result = dot3(stream, ordered)
        out[:, at : at + result.shape[1]] = result * scale if scale != 1.0 else result
        at += result.shape[1]


def attend_kernel(q_ref, *refs):
    pieces, out = refs[:-1], refs[-1]
    heads_width = q_ref.shape[1]
    for head in range(heads_width // DH):
        cols = slice(head * DH, (head + 1) * DH)
        vcols = slice(heads_width + head * DH, heads_width + (head + 1) * DH)
        query = q_ref[:, cols]
        keys = jnp.concatenate([piece[:, cols] for piece in pieces], 0)
        values = jnp.concatenate([piece[:, vcols] for piece in pieces], 0)
        scores = dot3(query, keys, ((1,), (1,)))
        top = jnp.max(scores, axis=1, keepdims=True)
        weights = jnp.exp(scores - top)
        total = jnp.sum(weights, axis=1, keepdims=True)
        out[:, cols] = dot3(weights, values) / total


def normalise(x, gain, bias):
    centre = jnp.mean(x, axis=-1, keepdims=True)
    spread = x - centre
    variance = jnp.mean(spread * spread, axis=-1, keepdims=True)
    return spread * lax.rsqrt(variance + EPS) * gain + bias


def gelu(v):
    return 0.5 * v * (1.0 + lax.erf(v * (1.0 / math.sqrt(2.0))))


def post_kernel(count, *refs):
    pos = lax.axis_index("head")
    mixed, emb = refs[:count], refs[count : 2 * count]
    weight, gain, bias, w_in, w_out = refs[2 * count : 2 * count + 5]
    outs = refs[2 * count + 5 :]
    stream = jnp.concatenate([m[...] for m in mixed], 1)
    attention = dot3(stream, weight[...])
    embedded = jnp.concatenate(butterfly([e[...] for e in emb], pos), 1)
    normed = normalise(embedded + attention, gain[...], bias[...])
    hidden = gelu(dot3(normed, w_in[...]))
    partial = butterfly(columns(dot3(hidden, w_out[...]), count), pos)
    mine = butterfly(columns(normed, count), pos)[0]
    outs[0][...] = mine + partial[0]
    for ref, block in zip(outs[1:], partial[1:]):
        ref[...] = block


def stats_kernel(count, *refs):
    parts, out, stats = refs[:count], refs[count], refs[count + 1]
    total = parts[0][...]
    for part in parts[1:]:
        total = total + part[...]
    flipped = total.T
    centre = jnp.mean(flipped, axis=0, keepdims=True)
    spread = flipped - centre
    out[...] = flipped
    stats[...] = jnp.concatenate([centre, jnp.sum(spread * spread, axis=0, keepdims=True)], 0)


def final_kernel(count, x_ref, *refs):
    pos = lax.axis_index("head")
    stats, gain, bias, out = refs[:count], refs[count], refs[count + 1], refs[count + 2]
    width = x_ref.shape[0]
    centres = [s[0:1, :] for s in stats]
    centre = sum(centres[1:], centres[0]) * (1.0 / count)
    square = sum((s[1:2, :] for s in stats[1:]), stats[0][1:2, :])
    for each in centres:
        square = square + width * (each - centre) * (each - centre)
    scale = lax.rsqrt(square * (1.0 / (count * width)) + EPS)
    pair = jnp.concatenate([gain[pos], bias[pos], jnp.zeros((6, width), F32)], 0).T
    out[...] = (x_ref[...] - centre) * scale * pair[:, 0:1] + pair[:, 1:2]


def send(x, axis, offset):
    size = lax.axis_size(axis)
    return lax.ppermute(x, axis, [(i, i ^ offset) for i in range(size)])


def spread_out(x, axis):
    return [x] + [send(x, axis, k) for k in range(1, lax.axis_size(axis))]


def hand_out(parts, axis):
    return [parts[0]] + [send(parts[k], axis, k) for k in range(1, lax.axis_size(axis))]


def gather_pieces(piece):
    size = lax.axis_size("var")
    if size > 8:
        return [lax.all_gather(piece, "var", axis=0, tiled=True)]
    far = [piece] + [send(piece, "var", k) for k in range(2, size, 2)]
    return far + [send(each, "var", 1) for each in far]


def on_device(
    series, emb_weight, emb_bias, q_weight, k_weight, v_weight, out_weight,
    norm1_gain, norm1_bias, ffn_in, ffn_out, norm2_gain, norm2_bias,
):
    n = lax.axis_size("head")
    rows, _ = series.shape
    model = emb_weight.shape[1]
    width = model // n
    heads_width = q_weight.shape[1]
    block = shape(rows, width)

    var_bits = lax.axis_size("var").bit_length() - 1
    bits = [var_bits - 1, 0]
    far = embed_half(n, True, series, emb_weight)
    near = embed_half(n, False, series, emb_weight)
    parts = [*near, *far]
    got = hand_out(parts, "head")
    cut = call(functools.partial(cut_kernel, bits), shape(heads_width >> len(bits), model))(out_weight)
    rest = jnp.stack(spread_out(cut, "head")[1:])[None]
    mine = call(functools.partial(embed_reduce_kernel, n), block)(
        *got, emb_bias.reshape(n, 1, width)
    )
    emb = spread_out(mine, "head")
    for bit in bits:
        rest = jnp.concatenate([rest, send(rest, "var", 1 << bit)], 0)
    pair = call(functools.partial(project_kernel, n, 1.0), shape(rows, 2 * heads_width))(*emb, k_weight, v_weight)
    queries = call(functools.partial(project_kernel, n, 1.0 / math.sqrt(DH)), shape(rows, heads_width))(*emb, q_weight)
    pieces = gather_pieces(pair)
    order = functools.partial(order_kernel, bits)
    whole_out = call(order, shape(n * heads_width, model))(out_weight, rest)
    mixed = call(attend_kernel, shape(rows, heads_width), limit=16)(queries, *pieces)
    mixes = spread_out(mixed, "head")
    partial = call(functools.partial(post_kernel, n), [block] * n, limit=16)(
        *mixes, *emb, whole_out, norm1_gain[None, :], norm1_bias[None, :], ffn_in, ffn_out
    )
    got = hand_out(partial, "head")
    flipped, stats = call(functools.partial(stats_kernel, n), [shape(width, rows), shape(2, rows)])(*got)
    return call(functools.partial(final_kernel, n), shape(width, rows))(
        flipped, *spread_out(stats, "head"), norm2_gain.reshape(n, 1, width), norm2_bias.reshape(n, 1, width)
    )


def solution(mesh):
    return jax.shard_map(
        on_device,
        mesh=mesh,
        in_specs=(
            P("var", "head"), P("head", None), P(), P(None, "head"), P(None, "head"), P(None, "head"),
            P("head", None), P(), P(), P(None, "head"), P("head", None), P(), P(),
        ),
        out_specs=P("head", "var"),
        check_vma=False,
    )
```

```python
import functools
import math

import jax
import jax.numpy as jnp
from jax import lax
from jax.experimental import pallas as pl
from jax.experimental.pallas import tpu as pltpu
from jax.sharding import PartitionSpec as P


DH = 64
EPS = 1e-05
F32 = jnp.float32
BF16 = jnp.bfloat16
MIB = 1 << 20


def split(x):
    hi = x.astype(BF16)
    return hi, (x - hi.astype(F32)).astype(BF16)


def mm(a, b, dims):
    return lax.dot_general(a, b, (dims, ((), ())), preferred_element_type=F32)


def dot3(a, b, dims=((1,), (0,))):
    a_hi, a_lo = split(a)
    b_hi, b_lo = split(b)
    rows = a.shape[0]
    first = mm(jnp.concatenate([a_hi, a_lo], 0), b_hi, dims)
    return first[:rows] + (first[rows:] + mm(a_hi, b_lo, dims))


def butterfly(blocks, pos):
    count = len(blocks)
    out = list(blocks)
    bit = 1
    while bit < count:
        take = (pos & bit) != 0
        out = [jnp.where(take, out[j ^ bit], out[j]) for j in range(count)]
        bit *= 2
    return out


def columns(x, count):
    width = x.shape[1] // count
    return [x[:, j * width : (j + 1) * width] for j in range(count)]


def call(body, outs, scratch=(), limit=12, grid=None, in_specs=None, out_specs=None, flops=0, nbytes=0):
    kwargs = {}
    if grid is not None:
        kwargs = dict(grid=grid, in_specs=in_specs, out_specs=out_specs)
    return pl.pallas_call(
        body,
        out_shape=outs,
        scratch_shapes=list(scratch),
        compiler_params=pltpu.CompilerParams(vmem_limit_bytes=limit * MIB),
        cost_estimate=pl.CostEstimate(flops=flops, bytes_accessed=nbytes, transcendentals=0),
        **kwargs,
    )


def shape(*dims):
    return jax.ShapeDtypeStruct(dims, F32)


def embed_kernel(count, x_hbm, w_hbm, *rest):
    outs, (x_buf, w_buf, x_sems, w_sems) = rest[:count], rest[count:]
    pos = lax.axis_index("head")
    steps, step = w_buf.shape[0], w_buf.shape[1]
    halves, wide = x_buf.shape[0], x_buf.shape[2]
    x_copies = [
        pltpu.make_async_copy(x_hbm.at[:, pl.ds(at * wide, wide)], x_buf.at[at], x_sems.at[at]) for at in range(halves)
    ]
    w_copies = [
        pltpu.make_async_copy(w_hbm.at[pl.ds(at * step, step), :], w_buf.at[at], w_sems.at[at]) for at in range(steps)
    ]
    for at in range(steps):
        if (at * step) % wide == 0:
            x_copies[at * step // wide].start()
        w_copies[at].start()
    total = None
    for at in range(steps):
        half, start = divmod(at * step, wide)
        if start == 0:
            x_copies[half].wait()
        w_copies[at].wait()
        part = dot3(x_buf[half, :, start : start + step], w_buf[at])
        total = part if total is None else total + part
    for ref, block in zip(outs, butterfly(columns(total, count), pos)):
        ref[...] = block


def embed(count, series, emb_weight):
    rows, depth = series.shape
    model = emb_weight.shape[1]
    step = math.gcd(depth, 256)
    steps = depth // step
    halves = 2 if steps % 2 == 0 else 1
    hbm = pl.BlockSpec(memory_space=pltpu.HBM)
    return pl.pallas_call(
        functools.partial(embed_kernel, count),
        out_shape=[shape(rows, model // count)] * count,
        in_specs=[hbm, hbm],
        scratch_shapes=[
            pltpu.VMEM((halves, rows, depth // halves), F32),
            pltpu.VMEM((steps, step, model), F32),
            pltpu.SemaphoreType.DMA((halves,)),
            pltpu.SemaphoreType.DMA((steps,)),
        ],
        name="embed",
        compiler_params=pltpu.CompilerParams(vmem_limit_bytes=122 * MIB // 2),
        cost_estimate=pl.CostEstimate(
            flops=6 * rows * depth * model, bytes_accessed=4 * depth * (model + rows), transcendentals=0
        ),
    )(series, emb_weight)


def piece_of(index, bits):
    return sum(((index >> bit) & 1) << at for at, bit in enumerate(bits))


def cut_kernel(bits, w_ref, out):
    part = piece_of(lax.axis_index("var"), bits)
    size = out.shape[0]
    out[...] = w_ref[pl.ds(pl.multiple_of(part * size, size), size), :]


def order_kernel(bits, own_ref, rest_ref, out):
    me = piece_of(lax.axis_index("var"), bits)
    rows = own_ref.shape[0]
    size = rows >> len(bits)
    out[0:rows, :] = own_ref[...]
    for apart in range(1 << len(bits)):
        for k in range(rest_ref.shape[1]):
            start = pl.multiple_of((k + 1) * rows + (me ^ apart) * size, size)
            out[pl.ds(start, size), :] = rest_ref[apart, k]


def bias_kernel(x_ref, bias, out):
    out[...] = x_ref[...] + bias[lax.axis_index("head")]


def add_kernel(*refs):
    total = refs[0][...]
    for part in refs[1:-1]:
        total = total + part[...]
    refs[-1][...] = total


def rows_of(weight, block, width):
    return weight[pl.ds(pl.multiple_of(block * width, width), width), :]


def project_kernel(count, scale, *refs):
    pos = lax.axis_index("head")
    blocks, weights, out = refs[:count], refs[count:-1], refs[-1]
    width = blocks[0].shape[1]
    stream = jnp.concatenate([block[...] for block in blocks], 1)
    at = 0
    for weight in weights:
        ordered = jnp.concatenate([rows_of(weight, pos ^ k, width) for k in range(count)], 0)
        result = dot3(stream, ordered)
        out[:, at : at + result.shape[1]] = result * scale if scale != 1.0 else result
        at += result.shape[1]


def attend_kernel(q_ref, *refs):
    pieces, out = refs[:-1], refs[-1]
    heads_width = q_ref.shape[1]
    for head in range(heads_width // DH):
        cols = slice(head * DH, (head + 1) * DH)
        vcols = slice(heads_width + head * DH, heads_width + (head + 1) * DH)
        query = q_ref[:, cols]
        keys = jnp.concatenate([piece[:, cols] for piece in pieces], 0)
        values = jnp.concatenate([piece[:, vcols] for piece in pieces], 0)
        scores = dot3(query, keys, ((1,), (1,)))
        top = jnp.max(scores, axis=1, keepdims=True)
        weights = jnp.exp(scores - top)
        total = jnp.sum(weights, axis=1, keepdims=True)
        out[:, cols] = dot3(weights, values) / total


def normalise(x, gain, bias):
    centre = jnp.mean(x, axis=-1, keepdims=True)
    spread = x - centre
    variance = jnp.mean(spread * spread, axis=-1, keepdims=True)
    return spread * lax.rsqrt(variance + EPS) * gain + bias


def gelu(v):
    return 0.5 * v * (1.0 + lax.erf(v * (1.0 / math.sqrt(2.0))))


def post_kernel(count, *refs):
    pos = lax.axis_index("head")
    mixed, emb = refs[:count], refs[count : 2 * count]
    weight, gain, bias, w_in, w_out = refs[2 * count : 2 * count + 5]
    outs = refs[2 * count + 5 :]
    stream = jnp.concatenate([m[...] for m in mixed], 1)
    attention = dot3(stream, weight[...])
    embedded = jnp.concatenate(butterfly([e[...] for e in emb], pos), 1)
    normed = normalise(embedded + attention, gain[...], bias[...])
    hidden = gelu(dot3(normed, w_in[...]))
    partial = butterfly(columns(dot3(hidden, w_out[...]), count), pos)
    mine = butterfly(columns(normed, count), pos)[0]
    outs[0][...] = mine + partial[0]
    for ref, block in zip(outs[1:], partial[1:]):
        ref[...] = block


def stats_kernel(count, *refs):
    parts, out, stats = refs[:count], refs[count], refs[count + 1]
    total = parts[0][...]
    for part in parts[1:]:
        total = total + part[...]
    flipped = total.T
    centre = jnp.mean(flipped, axis=0, keepdims=True)
    spread = flipped - centre
    out[...] = flipped
    stats[...] = jnp.concatenate([centre, jnp.sum(spread * spread, axis=0, keepdims=True)], 0)


def final_kernel(count, x_ref, *refs):
    pos = lax.axis_index("head")
    stats, gain, bias, out = refs[:count], refs[count], refs[count + 1], refs[count + 2]
    width = x_ref.shape[0]
    centres = [s[0:1, :] for s in stats]
    centre = sum(centres[1:], centres[0]) * (1.0 / count)
    square = sum((s[1:2, :] for s in stats[1:]), stats[0][1:2, :])
    for each in centres:
        square = square + width * (each - centre) * (each - centre)
    scale = lax.rsqrt(square * (1.0 / (count * width)) + EPS)
    pair = jnp.concatenate([gain[pos], bias[pos], jnp.zeros((6, width), F32)], 0).T
    out[...] = (x_ref[...] - centre) * scale * pair[:, 0:1] + pair[:, 1:2]


def send(x, axis, offset):
    size = lax.axis_size(axis)
    return lax.ppermute(x, axis, [(i, i ^ offset) for i in range(size)])


def spread_out(x, axis):
    return [x] + [send(x, axis, k) for k in range(1, lax.axis_size(axis))]


def hand_out(parts, axis):
    return [parts[0]] + [send(parts[k], axis, k) for k in range(1, lax.axis_size(axis))]


def gather_pieces(piece):
    size = lax.axis_size("var")
    if size > 8:
        return [lax.all_gather(piece, "var", axis=0, tiled=True)]
    far = [piece] + [send(piece, "var", k) for k in range(2, size, 2)]
    return far + [send(each, "var", 1) for each in far]


def on_device(
    series, emb_weight, emb_bias, q_weight, k_weight, v_weight, out_weight,
    norm1_gain, norm1_bias, ffn_in, ffn_out, norm2_gain, norm2_bias,
):
    n = lax.axis_size("head")
    rows, _ = series.shape
    model = emb_weight.shape[1]
    width = model // n
    heads_width = q_weight.shape[1]
    block = shape(rows, width)

    var_bits = lax.axis_size("var").bit_length() - 1
    bits = [var_bits - 1, 0]
    parts = embed(n, series, emb_weight)
    got = hand_out(parts, "head")
    got[0] = call(bias_kernel, block)(parts[0], emb_bias.reshape(n, 1, width))
    cut = call(functools.partial(cut_kernel, bits), shape(heads_width >> len(bits), model))(out_weight)
    rest = jnp.stack(spread_out(cut, "head")[1:])[None]
    mine = call(add_kernel, block)(*got)
    emb = spread_out(mine, "head")
    for bit in bits:
        rest = jnp.concatenate([rest, send(rest, "var", 1 << bit)], 0)
    pair = call(functools.partial(project_kernel, n, 1.0), shape(rows, 2 * heads_width))(*emb, k_weight, v_weight)
    queries = call(functools.partial(project_kernel, n, 1.0 / math.sqrt(DH)), shape(rows, heads_width))(*emb, q_weight)
    pieces = gather_pieces(pair)
    order = functools.partial(order_kernel, bits)
    whole_out = call(order, shape(n * heads_width, model))(out_weight, rest)
    mixed = call(attend_kernel, shape(rows, heads_width), limit=16)(queries, *pieces)
    mixes = spread_out(mixed, "head")
    partial = call(functools.partial(post_kernel, n), [block] * n, limit=16)(
        *mixes, *emb, whole_out, norm1_gain[None, :], norm1_bias[None, :], ffn_in, ffn_out
    )
    got = hand_out(partial, "head")
    flipped, stats = call(functools.partial(stats_kernel, n), [shape(width, rows), shape(2, rows)])(*got)
    return call(functools.partial(final_kernel, n), shape(width, rows))(
        flipped, *spread_out(stats, "head"), norm2_gain.reshape(n, 1, width), norm2_bias.reshape(n, 1, width)
    )


def solution(mesh):
    return jax.shard_map(
        on_device,
        mesh=mesh,
        in_specs=(
            P("var", "head"), P("head", None), P(), P(None, "head"), P(None, "head"), P(None, "head"),
            P("head", None), P(), P(), P(None, "head"), P("head", None), P(), P(),
        ),
        out_specs=P("head", "var"),
        check_vma=False,
    )
```

```python
import functools
import math

import jax
import jax.numpy as jnp
from jax import lax
from jax.experimental import pallas as pl
from jax.experimental.pallas import tpu as pltpu
from jax.sharding import PartitionSpec as P


DH = 64
EPS = 1e-05
F32 = jnp.float32
BF16 = jnp.bfloat16
MIB = 1 << 20


def split(x):
    hi = x.astype(BF16)
    return hi, (x - hi.astype(F32)).astype(BF16)


def mm(a, b, dims):
    return lax.dot_general(a, b, (dims, ((), ())), preferred_element_type=F32)


def dot3(a, b, dims=((1,), (0,))):
    a_hi, a_lo = split(a)
    b_hi, b_lo = split(b)
    rows = a.shape[0]
    first = mm(jnp.concatenate([a_hi, a_lo], 0), b_hi, dims)
    return first[:rows] + (first[rows:] + mm(a_hi, b_lo, dims))


def butterfly(blocks, pos):
    count = len(blocks)
    out = list(blocks)
    bit = 1
    while bit < count:
        take = (pos & bit) != 0
        out = [jnp.where(take, out[j ^ bit], out[j]) for j in range(count)]
        bit *= 2
    return out


def columns(x, count):
    width = x.shape[1] // count
    return [x[:, j * width : (j + 1) * width] for j in range(count)]


def call(body, outs, scratch=(), limit=12, grid=None, in_specs=None, out_specs=None, flops=0, nbytes=0):
    kwargs = {}
    if grid is not None:
        kwargs = dict(grid=grid, in_specs=in_specs, out_specs=out_specs)
    return pl.pallas_call(
        body,
        out_shape=outs,
        scratch_shapes=list(scratch),
        compiler_params=pltpu.CompilerParams(vmem_limit_bytes=limit * MIB),
        cost_estimate=pl.CostEstimate(flops=flops, bytes_accessed=nbytes, transcendentals=0),
        **kwargs,
    )


def shape(*dims):
    return jax.ShapeDtypeStruct(dims, F32)


def embed_kernel(count, x_hbm, w_hbm, *rest):
    outs, (x_buf, w_buf, x_sems, w_sems) = rest[:count], rest[count:]
    pos = lax.axis_index("head")
    steps, step = w_buf.shape[0], w_buf.shape[1]
    halves, wide = x_buf.shape[0], x_buf.shape[2]
    x_copies = [
        pltpu.make_async_copy(x_hbm.at[:, pl.ds(at * wide, wide)], x_buf.at[at], x_sems.at[at]) for at in range(halves)
    ]
    w_copies = [
        pltpu.make_async_copy(w_hbm.at[pl.ds(at * step, step), :], w_buf.at[at], w_sems.at[at]) for at in range(steps)
    ]
    for at in range(steps):
        if (at * step) % wide == 0:
            x_copies[at * step // wide].start()
        w_copies[at].start()
    total = None
    for at in range(steps):
        half, start = divmod(at * step, wide)
        if start == 0:
            x_copies[half].wait()
        w_copies[at].wait()
        part = dot3(x_buf[half, :, start : start + step], w_buf[at])
        total = part if total is None else total + part
    for ref, block in zip(outs, butterfly(columns(total, count), pos)):
        ref[...] = block


def embed(count, series, emb_weight):
    rows, depth = series.shape
    model = emb_weight.shape[1]
    step = math.gcd(depth, 512)
    steps = depth // step
    halves = 2 if steps % 2 == 0 else 1
    hbm = pl.BlockSpec(memory_space=pltpu.HBM)
    return pl.pallas_call(
        functools.partial(embed_kernel, count),
        out_shape=[shape(rows, model // count)] * count,
        in_specs=[hbm, hbm],
        scratch_shapes=[
            pltpu.VMEM((halves, rows, depth // halves), F32),
            pltpu.VMEM((steps, step, model), F32),
            pltpu.SemaphoreType.DMA((halves,)),
            pltpu.SemaphoreType.DMA((steps,)),
        ],
        name="embed",
        compiler_params=pltpu.CompilerParams(vmem_limit_bytes=122 * MIB // 2),
        cost_estimate=pl.CostEstimate(
            flops=6 * rows * depth * model, bytes_accessed=4 * depth * (model + rows), transcendentals=0
        ),
    )(series, emb_weight)


def piece_of(index, bits):
    return sum(((index >> bit) & 1) << at for at, bit in enumerate(bits))


def cut_kernel(bits, w_ref, out):
    part = piece_of(lax.axis_index("var"), bits)
    size = out.shape[0]
    out[...] = w_ref[pl.ds(pl.multiple_of(part * size, size), size), :]


def order_kernel(bits, own_ref, rest_ref, out):
    me = piece_of(lax.axis_index("var"), bits)
    rows = own_ref.shape[0]
    size = rows >> len(bits)
    out[0:rows, :] = own_ref[...]
    for apart in range(1 << len(bits)):
        for k in range(rest_ref.shape[1]):
            start = pl.multiple_of((k + 1) * rows + (me ^ apart) * size, size)
            out[pl.ds(start, size), :] = rest_ref[apart, k]


def bias_kernel(x_ref, bias, out):
    out[...] = x_ref[...] + bias[lax.axis_index("head")]


def add_kernel(*refs):
    total = refs[0][...]
    for part in refs[1:-1]:
        total = total + part[...]
    refs[-1][...] = total


def rows_of(weight, block, width):
    return weight[pl.ds(pl.multiple_of(block * width, width), width), :]


def project_kernel(count, scale, *refs):
    pos = lax.axis_index("head")
    blocks, weights, out = refs[:count], refs[count:-1], refs[-1]
    width = blocks[0].shape[1]
    stream = jnp.concatenate([block[...] for block in blocks], 1)
    at = 0
    for weight in weights:
        ordered = jnp.concatenate([rows_of(weight, pos ^ k, width) for k in range(count)], 0)
        result = dot3(stream, ordered)
        out[:, at : at + result.shape[1]] = result * scale if scale != 1.0 else result
        at += result.shape[1]


def attend_kernel(q_ref, *refs):
    pieces, out = refs[:-1], refs[-1]
    heads_width = q_ref.shape[1]
    for head in range(heads_width // DH):
        cols = slice(head * DH, (head + 1) * DH)
        vcols = slice(heads_width + head * DH, heads_width + (head + 1) * DH)
        query = q_ref[:, cols]
        keys = jnp.concatenate([piece[:, cols] for piece in pieces], 0)
        values = jnp.concatenate([piece[:, vcols] for piece in pieces], 0)
        scores = dot3(query, keys, ((1,), (1,)))
        top = jnp.max(scores, axis=1, keepdims=True)
        weights = jnp.exp(scores - top)
        total = jnp.sum(weights, axis=1, keepdims=True)
        out[:, cols] = dot3(weights, values) / total


def normalise(x, gain, bias):
    centre = jnp.mean(x, axis=-1, keepdims=True)
    spread = x - centre
    variance = jnp.mean(spread * spread, axis=-1, keepdims=True)
    return spread * lax.rsqrt(variance + EPS) * gain + bias


def gelu(v):
    return 0.5 * v * (1.0 + lax.erf(v * (1.0 / math.sqrt(2.0))))


def post_kernel(count, *refs):
    pos = lax.axis_index("head")
    mixed, emb = refs[:count], refs[count : 2 * count]
    weight, gain, bias, w_in, w_out = refs[2 * count : 2 * count + 5]
    outs = refs[2 * count + 5 :]
    stream = jnp.concatenate([m[...] for m in mixed], 1)
    attention = dot3(stream, weight[...])
    embedded = jnp.concatenate(butterfly([e[...] for e in emb], pos), 1)
    normed = normalise(embedded + attention, gain[...], bias[...])
    hidden = gelu(dot3(normed, w_in[...]))
    partial = butterfly(columns(dot3(hidden, w_out[...]), count), pos)
    partial[0] = partial[0] + butterfly(columns(normed, count), pos)[0]
    store_halves(partial, outs)


def store_halves(blocks, outs):
    outs[0][...] = jnp.concatenate(blocks[::2], 1)
    outs[1][...] = jnp.concatenate(blocks[1::2], 1)


def halve_kernel(count, kept, got, *outs):
    total = kept[...] + got[...]
    if len(outs) == 1:
        outs[0][...] = total
    else:
        store_halves(columns(total, count), outs)


def stats_kernel(kept, got, out, stats):
    width = out.shape[0]
    other = jnp.concatenate([got[:, width:], got[:, :width]], 1)
    flipped = (kept[...] + other).T
    centre = jnp.mean(flipped, axis=0, keepdims=True)
    spread = flipped - centre
    out[...] = flipped[:width]
    stats[...] = jnp.concatenate([centre, jnp.sum(spread * spread, axis=0, keepdims=True)], 0)


def final_kernel(share, x_ref, *refs):
    pos = lax.axis_index("head")
    stats, (gain, bias, out) = refs[:-3], refs[-3:]
    width = x_ref.shape[0]
    centres = [s[0:1, :] for s in stats]
    centre = sum(centres[1:], centres[0]) * (1.0 / len(stats))
    square = sum((s[1:2, :] for s in stats[1:]), stats[0][1:2, :])
    for each in centres:
        square = square + share * (each - centre) * (each - centre)
    scale = lax.rsqrt(square * (1.0 / (len(stats) * share)) + EPS)
    pair = jnp.concatenate([gain[pos], bias[pos], jnp.zeros((6, width), F32)], 0).T
    out[...] = (x_ref[...] - centre) * scale * pair[:, 0:1] + pair[:, 1:2]


def send(x, axis, offset):
    size = lax.axis_size(axis)
    return lax.ppermute(x, axis, [(i, i ^ offset) for i in range(size)])


def spread_out(x, axis):
    return [x] + [send(x, axis, k) for k in range(1, lax.axis_size(axis))]


def hand_out(parts, axis):
    return [parts[0]] + [send(parts[k], axis, k) for k in range(1, lax.axis_size(axis))]


def bits_below(count):
    return [1 << at for at in range(count.bit_length() - 1)]


def halving(kept, give, count):
    left = count // 2
    for bit in bits_below(count // 2):
        got = send(give, "head", bit)
        rows, wide = kept.shape
        last = left == 2
        outs = shape(rows, wide) if last else [shape(rows, wide // 2)] * 2
        result = call(functools.partial(halve_kernel, left), outs)(kept, got)
        kept, give = (result, None) if last else result
        left //= 2
    return kept


def gather_pieces(piece):
    size = lax.axis_size("var")
    if size > 8:
        return [lax.all_gather(piece, "var", axis=0, tiled=True)]
    far = [piece] + [send(piece, "var", k) for k in range(2, size, 2)]
    return far + [send(each, "var", 1) for each in far]


def on_device(
    series, emb_weight, emb_bias, q_weight, k_weight, v_weight, out_weight,
    norm1_gain, norm1_bias, ffn_in, ffn_out, norm2_gain, norm2_bias,
):
    n = lax.axis_size("head")
    rows, _ = series.shape
    model = emb_weight.shape[1]
    width = model // n
    heads_width = q_weight.shape[1]
    block = shape(rows, width)

    var_bits = lax.axis_size("var").bit_length() - 1
    bits = [var_bits - 1, 0]
    parts = embed(n, series, emb_weight)
    got = hand_out(parts, "head")
    got[0] = call(bias_kernel, block)(parts[0], emb_bias.reshape(n, 1, width))
    cut = call(functools.partial(cut_kernel, bits), shape(heads_width >> len(bits), model))(out_weight)
    rest = jnp.stack(spread_out(cut, "head")[1:])[None]
    mine = call(add_kernel, block)(*got)
    emb = spread_out(mine, "head")
    for bit in bits:
        rest = jnp.concatenate([rest, send(rest, "var", 1 << bit)], 0)
    pair = call(functools.partial(project_kernel, n, 1.0), shape(rows, 2 * heads_width))(*emb, k_weight, v_weight)
    queries = call(functools.partial(project_kernel, n, 1.0 / math.sqrt(DH)), shape(rows, heads_width))(*emb, q_weight)
    pieces = gather_pieces(pair)
    order = functools.partial(order_kernel, bits)
    whole_out = call(order, shape(n * heads_width, model))(out_weight, rest)
    mixed = call(attend_kernel, shape(rows, heads_width), limit=16)(queries, *pieces)
    mixes = spread_out(mixed, "head")
    kept, give = call(functools.partial(post_kernel, n), [shape(rows, model // 2)] * 2, limit=16)(
        *mixes, *emb, whole_out, norm1_gain[None, :], norm1_bias[None, :], ffn_in, ffn_out
    )
    kept = halving(kept, give, n)
    got = send(kept, "head", n // 2)
    flipped, stats = call(stats_kernel, [shape(width, rows), shape(2, rows)])(kept, got)
    every = [stats]
    for bit in bits_below(n // 2):
        every += [send(each, "head", bit) for each in every]
    return call(functools.partial(final_kernel, 2 * width), shape(width, rows))(
        flipped, *every, norm2_gain.reshape(n, 1, width), norm2_bias.reshape(n, 1, width)
    )


def solution(mesh):
    return jax.shard_map(
        on_device,
        mesh=mesh,
        in_specs=(
            P("var", "head"), P("head", None), P(), P(None, "head"), P(None, "head"), P(None, "head"),
            P("head", None), P(), P(), P(None, "head"), P("head", None), P(), P(),
        ),
        out_specs=P("head", "var"),
        check_vma=False,
    )
```

```python
import functools
import math

import jax
import jax.numpy as jnp
from jax import lax
from jax.experimental import pallas as pl
from jax.experimental.pallas import tpu as pltpu
from jax.sharding import PartitionSpec as P


DH = 64
EPS = 1e-05
F32 = jnp.float32
BF16 = jnp.bfloat16
MIB = 1 << 20


def split(x):
    hi = x.astype(BF16)
    return hi, (x - hi.astype(F32)).astype(BF16)


def mm(a, b, dims):
    return lax.dot_general(a, b, (dims, ((), ())), preferred_element_type=F32)


def dot3(a, b, dims=((1,), (0,))):
    a_hi, a_lo = split(a)
    b_hi, b_lo = split(b)
    rows = a.shape[0]
    first = mm(jnp.concatenate([a_hi, a_lo], 0), b_hi, dims)
    return first[:rows] + (first[rows:] + mm(a_hi, b_lo, dims))


def butterfly(blocks, pos):
    count = len(blocks)
    out = list(blocks)
    bit = 1
    while bit < count:
        take = (pos & bit) != 0
        out = [jnp.where(take, out[j ^ bit], out[j]) for j in range(count)]
        bit *= 2
    return out


def columns(x, count):
    width = x.shape[1] // count
    return [x[:, j * width : (j + 1) * width] for j in range(count)]


def call(body, outs, scratch=(), limit=12, grid=None, in_specs=None, out_specs=None, flops=0, nbytes=0):
    kwargs = {}
    if grid is not None:
        kwargs = dict(grid=grid, in_specs=in_specs, out_specs=out_specs)
    return pl.pallas_call(
        body,
        out_shape=outs,
        scratch_shapes=list(scratch),
        compiler_params=pltpu.CompilerParams(vmem_limit_bytes=limit * MIB),
        cost_estimate=pl.CostEstimate(flops=flops, bytes_accessed=nbytes, transcendentals=0),
        **kwargs,
    )


def shape(*dims):
    return jax.ShapeDtypeStruct(dims, F32)


def embed_kernel(count, x_hbm, w_hbm, *rest):
    outs, (x_buf, w_buf, x_sems, w_sems) = rest[:count], rest[count:]
    pos = lax.axis_index("head")
    steps, step = w_buf.shape[0], w_buf.shape[1]
    halves, wide = x_buf.shape[0], x_buf.shape[2]
    x_copies = [
        pltpu.make_async_copy(x_hbm.at[:, pl.ds(at * wide, wide)], x_buf.at[at], x_sems.at[at]) for at in range(halves)
    ]
    w_copies = [
        pltpu.make_async_copy(w_hbm.at[pl.ds(at * step, step), :], w_buf.at[at], w_sems.at[at]) for at in range(steps)
    ]
    for at in range(steps):
        if (at * step) % wide == 0:
            x_copies[at * step // wide].start()
        w_copies[at].start()
    total = None
    for at in range(steps):
        half, start = divmod(at * step, wide)
        if start == 0:
            x_copies[half].wait()
        w_copies[at].wait()
        part = dot3(x_buf[half, :, start : start + step], w_buf[at])
        total = part if total is None else total + part
    for ref, block in zip(outs, butterfly(columns(total, count), pos)):
        ref[...] = block


def embed(count, series, emb_weight):
    rows, depth = series.shape
    model = emb_weight.shape[1]
    step = math.gcd(depth, 512)
    steps = depth // step
    halves = 2 if steps % 2 == 0 else 1
    hbm = pl.BlockSpec(memory_space=pltpu.HBM)
    return pl.pallas_call(
        functools.partial(embed_kernel, count),
        out_shape=[shape(rows, model // count)] * count,
        in_specs=[hbm, hbm],
        scratch_shapes=[
            pltpu.VMEM((halves, rows, depth // halves), F32),
            pltpu.VMEM((steps, step, model), F32),
            pltpu.SemaphoreType.DMA((halves,)),
            pltpu.SemaphoreType.DMA((steps,)),
        ],
        name="embed",
        compiler_params=pltpu.CompilerParams(vmem_limit_bytes=122 * MIB // 2),
        cost_estimate=pl.CostEstimate(
            flops=6 * rows * depth * model, bytes_accessed=4 * depth * (model + rows), transcendentals=0
        ),
    )(series, emb_weight)


def piece_of(index, bits):
    return sum(((index >> bit) & 1) << at for at, bit in enumerate(bits))


def cut_kernel(bits, w_ref, out):
    part = piece_of(lax.axis_index("var"), bits)
    size = out.shape[0]
    out[...] = w_ref[pl.ds(pl.multiple_of(part * size, size), size), :]


def order_kernel(bits, own_ref, rest_ref, out):
    me = piece_of(lax.axis_index("var"), bits)
    rows = own_ref.shape[0]
    size = rows >> len(bits)
    out[0:rows, :] = own_ref[...]
    for apart in range(1 << len(bits)):
        for k in range(rest_ref.shape[1]):
            start = pl.multiple_of((k + 1) * rows + (me ^ apart) * size, size)
            out[pl.ds(start, size), :] = rest_ref[apart, k]


def bias_kernel(x_ref, bias, out):
    out[...] = x_ref[...] + bias[lax.axis_index("head")]


def add_kernel(*refs):
    total = refs[0][...]
    for part in refs[1:-1]:
        total = total + part[...]
    refs[-1][...] = total


def rows_of(weight, block, width):
    return weight[pl.ds(pl.multiple_of(block * width, width), width), :]


def project_kernel(count, scale, *refs):
    pos = lax.axis_index("head")
    blocks, weights, out = refs[:count], refs[count:-1], refs[-1]
    width = blocks[0].shape[1]
    stream = jnp.concatenate([block[...] for block in blocks], 1)
    at = 0
    for weight in weights:
        ordered = jnp.concatenate([rows_of(weight, pos ^ k, width) for k in range(count)], 0)
        result = dot3(stream, ordered)
        out[:, at : at + result.shape[1]] = result * scale if scale != 1.0 else result
        at += result.shape[1]


def attend_kernel(q_ref, *refs):
    pieces, out = refs[:-1], refs[-1]
    heads_width = q_ref.shape[1]
    for head in range(heads_width // DH):
        cols = slice(head * DH, (head + 1) * DH)
        vcols = slice(heads_width + head * DH, heads_width + (head + 1) * DH)
        query = q_ref[:, cols]
        keys = jnp.concatenate([piece[:, cols] for piece in pieces], 0)
        values = jnp.concatenate([piece[:, vcols] for piece in pieces], 0)
        scores = dot3(query, keys, ((1,), (1,)))
        top = jnp.max(scores, axis=1, keepdims=True)
        weights = jnp.exp(scores - top)
        total = jnp.sum(weights, axis=1, keepdims=True)
        out[:, cols] = dot3(weights, values) / total


def normalise(x, gain, bias):
    centre = jnp.mean(x, axis=-1, keepdims=True)
    spread = x - centre
    variance = jnp.mean(spread * spread, axis=-1, keepdims=True)
    return spread * lax.rsqrt(variance + EPS) * gain + bias


def gelu(v):
    return 0.5 * v * (1.0 + lax.erf(v * (1.0 / math.sqrt(2.0))))


def post_kernel(count, *refs):
    pos = lax.axis_index("head")
    mixed, emb = refs[:count], refs[count : 2 * count]
    weight, gain, bias, w_in, w_out = refs[2 * count : 2 * count + 5]
    outs = refs[2 * count + 5 :]
    stream = jnp.concatenate([m[...] for m in mixed], 1)
    attention = dot3(stream, weight[...])
    embedded = jnp.concatenate(butterfly([e[...] for e in emb], pos), 1)
    normed = normalise(embedded + attention, gain[...], bias[...])
    hidden = gelu(dot3(normed, w_in[...]))
    partial = butterfly(columns(dot3(hidden, w_out[...]), count), pos)
    mine = butterfly(columns(normed, count), pos)[0]
    outs[0][...] = mine + partial[0]
    for ref, block in zip(outs[1:], partial[1:]):
        ref[...] = block


def stats_kernel(count, *refs):
    parts, out, stats = refs[:count], refs[count], refs[count + 1]
    total = parts[0][...]
    for part in parts[1:]:
        total = total + part[...]
    flipped = total.T
    centre = jnp.mean(flipped, axis=0, keepdims=True)
    spread = flipped - centre
    out[...] = flipped
    stats[...] = jnp.concatenate([centre, jnp.sum(spread * spread, axis=0, keepdims=True)], 0)


def final_kernel(count, x_ref, *refs):
    pos = lax.axis_index("head")
    stats, gain, bias, out = refs[:count], refs[count], refs[count + 1], refs[count + 2]
    width = x_ref.shape[0]
    centres = [s[0:1, :] for s in stats]
    centre = sum(centres[1:], centres[0]) * (1.0 / count)
    square = sum((s[1:2, :] for s in stats[1:]), stats[0][1:2, :])
    for each in centres:
        square = square + width * (each - centre) * (each - centre)
    scale = lax.rsqrt(square * (1.0 / (count * width)) + EPS)
    pair = jnp.concatenate([gain[pos], bias[pos], jnp.zeros((6, width), F32)], 0).T
    out[...] = (x_ref[...] - centre) * scale * pair[:, 0:1] + pair[:, 1:2]


def send(x, axis, offset):
    size = lax.axis_size(axis)
    return lax.ppermute(x, axis, [(i, i ^ offset) for i in range(size)])


def spread_out(x, axis):
    return [x] + [send(x, axis, k) for k in range(1, lax.axis_size(axis))]


def hand_out(parts, axis):
    return [parts[0]] + [send(parts[k], axis, k) for k in range(1, lax.axis_size(axis))]


def bits_below(count):
    return [1 << at for at in range(count.bit_length() - 1)]


def gather_pieces(piece):
    size = lax.axis_size("var")
    if size > 8:
        return [lax.all_gather(piece, "var", axis=0, tiled=True)]
    far = [piece] + [send(piece, "var", k) for k in range(2, size, 2)]
    return far + [send(each, "var", 1) for each in far]


def on_device(
    series, emb_weight, emb_bias, q_weight, k_weight, v_weight, out_weight,
    norm1_gain, norm1_bias, ffn_in, ffn_out, norm2_gain, norm2_bias,
):
    n = lax.axis_size("head")
    rows, _ = series.shape
    model = emb_weight.shape[1]
    width = model // n
    heads_width = q_weight.shape[1]
    block = shape(rows, width)

    var_bits = lax.axis_size("var").bit_length() - 1
    bits = [var_bits - 1, 0]
    parts = embed(n, series, emb_weight)
    got = hand_out(parts, "head")
    got[0] = call(bias_kernel, block)(parts[0], emb_bias.reshape(n, 1, width))
    cut = call(functools.partial(cut_kernel, bits), shape(heads_width >> len(bits), model))(out_weight)
    have = cut[None]
    for bit in bits_below(n):
        have = jnp.concatenate([have, send(have, "head", bit)], 0)
    rest = have[None, 1:]
    mine = call(add_kernel, block)(*got)
    emb = spread_out(mine, "head")
    for bit in bits:
        rest = jnp.concatenate([rest, send(rest, "var", 1 << bit)], 0)
    pair = call(functools.partial(project_kernel, n, 1.0), shape(rows, 2 * heads_width))(*emb, k_weight, v_weight)
    queries = call(functools.partial(project_kernel, n, 1.0 / math.sqrt(DH)), shape(rows, heads_width))(*emb, q_weight)
    pieces = gather_pieces(pair)
    order = functools.partial(order_kernel, bits)
    whole_out = call(order, shape(n * heads_width, model))(out_weight, rest)
    mixed = call(attend_kernel, shape(rows, heads_width), limit=16)(queries, *pieces)
    mixes = spread_out(mixed, "head")
    partial = call(functools.partial(post_kernel, n), [block] * n, limit=16)(
        *mixes, *emb, whole_out, norm1_gain[None, :], norm1_bias[None, :], ffn_in, ffn_out
    )
    got = hand_out(partial, "head")
    flipped, stats = call(functools.partial(stats_kernel, n), [shape(width, rows), shape(2, rows)])(*got)
    return call(functools.partial(final_kernel, n), shape(width, rows))(
        flipped, *spread_out(stats, "head"), norm2_gain.reshape(n, 1, width), norm2_bias.reshape(n, 1, width)
    )


def solution(mesh):
    return jax.shard_map(
        on_device,
        mesh=mesh,
        in_specs=(
            P("var", "head"), P("head", None), P(), P(None, "head"), P(None, "head"), P(None, "head"),
            P("head", None), P(), P(), P(None, "head"), P("head", None), P(), P(),
        ),
        out_specs=P("head", "var"),
        check_vma=False,
    )
```

```python
import functools
import math

import jax
import jax.numpy as jnp
from jax import lax
from jax.experimental import pallas as pl
from jax.experimental.pallas import tpu as pltpu
from jax.sharding import PartitionSpec as P


DH = 64
EPS = 1e-05
F32 = jnp.float32
BF16 = jnp.bfloat16
MIB = 1 << 20


def split(x):
    hi = x.astype(BF16)
    return hi, (x - hi.astype(F32)).astype(BF16)


def mm(a, b, dims):
    return lax.dot_general(a, b, (dims, ((), ())), preferred_element_type=F32)


def dot3_split(a, b_hi, b_lo, dims=((1,), (0,))):
    a_hi, a_lo = split(a)
    rows = a.shape[0]
    first = mm(jnp.concatenate([a_hi, a_lo], 0), b_hi, dims)
    return first[:rows] + (first[rows:] + mm(a_hi, b_lo, dims))


def dot3(a, b, dims=((1,), (0,))):
    return dot3_split(a, *split(b), dims)


def butterfly(blocks, pos):
    count = len(blocks)
    out = list(blocks)
    bit = 1
    while bit < count:
        take = (pos & bit) != 0
        out = [jnp.where(take, out[j ^ bit], out[j]) for j in range(count)]
        bit *= 2
    return out


def columns(x, count):
    width = x.shape[1] // count
    return [x[:, j * width : (j + 1) * width] for j in range(count)]


def call(body, outs, scratch=(), limit=12, grid=None, in_specs=None, out_specs=None, flops=0, nbytes=0):
    kwargs = {}
    if grid is not None:
        kwargs = dict(grid=grid, in_specs=in_specs, out_specs=out_specs)
    return pl.pallas_call(
        body,
        out_shape=outs,
        scratch_shapes=list(scratch),
        compiler_params=pltpu.CompilerParams(vmem_limit_bytes=limit * MIB),
        cost_estimate=pl.CostEstimate(flops=flops, bytes_accessed=nbytes, transcendentals=0),
        **kwargs,
    )


def shape(*dims, dtype=F32):
    return jax.ShapeDtypeStruct(dims, dtype)


def halves_of(*dims):
    return [shape(*dims, dtype=BF16)] * 2


def embed_kernel(count, x_hbm, w_hbm, *rest):
    outs, (x_buf, w_buf, x_sems, w_sems) = rest[:count], rest[count:]
    pos = lax.axis_index("head")
    steps, step = w_buf.shape[0], w_buf.shape[1]
    halves, wide = x_buf.shape[0], x_buf.shape[2]
    x_copies = [
        pltpu.make_async_copy(x_hbm.at[:, pl.ds(at * wide, wide)], x_buf.at[at], x_sems.at[at]) for at in range(halves)
    ]
    w_copies = [
        pltpu.make_async_copy(w_hbm.at[pl.ds(at * step, step), :], w_buf.at[at], w_sems.at[at]) for at in range(steps)
    ]
    for at in range(steps):
        if (at * step) % wide == 0:
            x_copies[at * step // wide].start()
        w_copies[at].start()
    total = None
    for at in range(steps):
        half, start = divmod(at * step, wide)
        if start == 0:
            x_copies[half].wait()
        w_copies[at].wait()
        part = dot3(x_buf[half, :, start : start + step], w_buf[at])
        total = part if total is None else total + part
    for ref, block in zip(outs, butterfly(columns(total, count), pos)):
        ref[...] = block


def embed(count, series, emb_weight):
    rows, depth = series.shape
    model = emb_weight.shape[1]
    step = math.gcd(depth, 512)
    steps = depth // step
    halves = 2 if steps % 2 == 0 else 1
    hbm = pl.BlockSpec(memory_space=pltpu.HBM)
    return pl.pallas_call(
        functools.partial(embed_kernel, count),
        out_shape=[shape(rows, model // count)] * count,
        in_specs=[hbm, hbm],
        scratch_shapes=[
            pltpu.VMEM((halves, rows, depth // halves), F32),
            pltpu.VMEM((steps, step, model), F32),
            pltpu.SemaphoreType.DMA((halves,)),
            pltpu.SemaphoreType.DMA((steps,)),
        ],
        name="embed",
        compiler_params=pltpu.CompilerParams(vmem_limit_bytes=126 * MIB // 2),
        cost_estimate=pl.CostEstimate(
            flops=6 * rows * depth * model, bytes_accessed=4 * depth * (model + rows), transcendentals=0
        ),
    )(series, emb_weight)


def piece_of(index, bits):
    return sum(((index >> bit) & 1) << at for at, bit in enumerate(bits))


def cut_kernel(bits, w_ref, out):
    part = piece_of(lax.axis_index("var"), bits)
    size = out.shape[0]
    out[...] = w_ref[pl.ds(pl.multiple_of(part * size, size), size), :]


def order_kernel(bits, own_ref, rest_ref, hi, lo):
    me = piece_of(lax.axis_index("var"), bits)
    rows = own_ref.shape[0]
    size = rows >> len(bits)
    hi[0:rows, :], lo[0:rows, :] = split(own_ref[...])
    for apart in range(1 << len(bits)):
        for k in range(rest_ref.shape[1]):
            at = pl.ds(pl.multiple_of((k + 1) * rows + (me ^ apart) * size, size), size)
            hi[at, :], lo[at, :] = split(rest_ref[apart, k])


def bias_kernel(x_ref, bias, out):
    out[...] = x_ref[...] + bias[lax.axis_index("head")]


def add_kernel(*refs):
    total = refs[0][...]
    for part in refs[1:-1]:
        total = total + part[...]
    refs[-1][...] = total


def split_kernel(*refs):
    count = len(refs) // 3
    for at in range(count):
        refs[count + 2 * at][...], refs[count + 2 * at + 1][...] = split(refs[at][...])


def ordered_kernel(count, k_ref, v_ref, q_ref, *outs):
    pos = lax.axis_index("head")
    width, cols = k_ref.shape[0] // count, k_ref.shape[1]
    for k in range(count):
        rows = pl.ds(pl.multiple_of((pos ^ k) * width, width), width)
        at = slice(k * width, (k + 1) * width)
        outs[0][at, :cols], outs[1][at, :cols] = split(k_ref[rows, :])
        outs[0][at, cols:], outs[1][at, cols:] = split(v_ref[rows, :])
        outs[2][at, :], outs[3][at, :] = split(q_ref[rows, :] * (1.0 / math.sqrt(DH)))


def project_kernel(*refs):
    blocks, hi, lo, out = refs[:-3], *refs[-3:]
    out[...] = dot3_split(jnp.concatenate([block[...] for block in blocks], 1), hi[...], lo[...])


def attend_kernel(q_ref, *refs, merge):
    if merge:
        (acc_a, top_a, sum_a), pieces, out = refs[:3], refs[3:-1], refs[-1]
    else:
        pieces, (acc_out, top_out, sum_out) = refs[:-3], refs[-3:]
    heads_width = q_ref.shape[1]
    for head in range(heads_width // DH):
        cols = slice(head * DH, (head + 1) * DH)
        vcols = slice(heads_width + head * DH, heads_width + (head + 1) * DH)
        query = q_ref[:, cols]
        keys = jnp.concatenate([piece[:, cols] for piece in pieces], 0)
        values = jnp.concatenate([piece[:, vcols] for piece in pieces], 0)
        scores = dot3(query, keys, ((1,), (1,)))
        top = jnp.max(scores, axis=1, keepdims=True)
        if merge:
            before = top_a[:, cols][:, :1]
            top = jnp.maximum(top, before)
        weights = jnp.exp(scores - top)
        total = jnp.sum(weights, axis=1, keepdims=True)
        acc = dot3(weights, values)
        if merge:
            fade = jnp.exp(before - top)
            out[:, cols] = (acc + acc_a[:, cols] * fade) / (total + sum_a[:, cols][:, :1] * fade)
        else:
            acc_out[:, cols] = acc
            top_out[:, cols] = jnp.broadcast_to(top, acc.shape)
            sum_out[:, cols] = jnp.broadcast_to(total, acc.shape)


def normalise(x, gain, bias):
    centre = jnp.mean(x, axis=-1, keepdims=True)
    spread = x - centre
    variance = jnp.mean(spread * spread, axis=-1, keepdims=True)
    return spread * lax.rsqrt(variance + EPS) * gain + bias


def gelu(v):
    return 0.5 * v * (1.0 + lax.erf(v * (1.0 / math.sqrt(2.0))))


def post_kernel(count, *refs):
    pos = lax.axis_index("head")
    mixed, emb = refs[:count], refs[count : 2 * count]
    o_hi, o_lo, gain, bias, in_hi, in_lo, out_hi, out_lo = refs[2 * count : 2 * count + 8]
    outs = refs[2 * count + 8 :]
    stream = jnp.concatenate([m[...] for m in mixed], 1)
    attention = dot3_split(stream, o_hi[...], o_lo[...])
    embedded = jnp.concatenate(butterfly([e[...] for e in emb], pos), 1)
    normed = normalise(embedded + attention, gain[...], bias[...])
    hidden = gelu(dot3_split(normed, in_hi[...], in_lo[...]))
    partial = butterfly(columns(dot3_split(hidden, out_hi[...], out_lo[...]), count), pos)
    mine = butterfly(columns(normed, count), pos)[0]
    outs[0][...] = mine + partial[0]
    for ref, block in zip(outs[1:], partial[1:]):
        ref[...] = block


def stats_kernel(count, *refs):
    parts, out, stats = refs[:count], refs[count], refs[count + 1]
    total = parts[0][...]
    for part in parts[1:]:
        total = total + part[...]
    flipped = total.T
    centre = jnp.mean(flipped, axis=0, keepdims=True)
    spread = flipped - centre
    out[...] = flipped
    stats[...] = jnp.concatenate([centre, jnp.sum(spread * spread, axis=0, keepdims=True)], 0)


def final_kernel(count, x_ref, *refs):
    pos = lax.axis_index("head")
    stats, gain, bias, out = refs[:count], refs[count], refs[count + 1], refs[count + 2]
    width = x_ref.shape[0]
    centres = [s[0:1, :] for s in stats]
    centre = sum(centres[1:], centres[0]) * (1.0 / count)
    square = sum((s[1:2, :] for s in stats[1:]), stats[0][1:2, :])
    for each in centres:
        square = square + width * (each - centre) * (each - centre)
    scale = lax.rsqrt(square * (1.0 / (count * width)) + EPS)
    pair = jnp.concatenate([gain[pos], bias[pos], jnp.zeros((6, width), F32)], 0).T
    out[...] = (x_ref[...] - centre) * scale * pair[:, 0:1] + pair[:, 1:2]


def send(x, axis, offset):
    size = lax.axis_size(axis)
    return lax.ppermute(x, axis, [(i, i ^ offset) for i in range(size)])


def spread_out(x, axis):
    return [x] + [send(x, axis, k) for k in range(1, lax.axis_size(axis))]


def hand_out(parts, axis):
    return [parts[0]] + [send(parts[k], axis, k) for k in range(1, lax.axis_size(axis))]


def bits_below(count):
    return [1 << at for at in range(count.bit_length() - 1)]


def gather_pieces(piece):
    size = lax.axis_size("var")
    if size > 8:
        whole = lax.all_gather(piece, "var", axis=0, tiled=True)
        cut = whole.shape[0] // 2
        return [whole[:cut]], [whole[cut:]]
    far = [piece] + [send(piece, "var", k) for k in range(2, size, 2)]
    near = [send(each, "var", 1) for each in far]
    return far + near[:1], near[1:]


def on_device(
    series, emb_weight, emb_bias, q_weight, k_weight, v_weight, out_weight,
    norm1_gain, norm1_bias, ffn_in, ffn_out, norm2_gain, norm2_bias,
):
    n = lax.axis_size("head")
    rows, _ = series.shape
    model = emb_weight.shape[1]
    width = model // n
    heads_width = q_weight.shape[1]
    block = shape(rows, width)

    var_bits = lax.axis_size("var").bit_length() - 1
    bits = [var_bits - 1, 0]
    parts = embed(n, series, emb_weight)
    got = hand_out(parts, "head")
    got[0] = call(bias_kernel, block)(parts[0], emb_bias.reshape(n, 1, width))
    cut = call(functools.partial(cut_kernel, bits), shape(heads_width >> len(bits), model))(out_weight)
    have = cut[None]
    for bit in bits_below(n):
        have = jnp.concatenate([have, send(have, "head", bit)], 0)
    rest = have[None, 1:]
    mine = call(add_kernel, block)(*got)
    emb = spread_out(mine, "head")
    for bit in bits:
        rest = jnp.concatenate([rest, send(rest, "var", 1 << bit)], 0)
    wide = halves_of(model, 2 * heads_width) + halves_of(model, heads_width)
    kv_hi, kv_lo, q_hi, q_lo = call(functools.partial(ordered_kernel, n), wide)(k_weight, v_weight, q_weight)
    pair = call(project_kernel, shape(rows, 2 * heads_width))(*emb, kv_hi, kv_lo)
    queries = call(project_kernel, shape(rows, heads_width))(*emb, q_hi, q_lo)
    first, later = gather_pieces(pair)
    ffn = call(split_kernel, halves_of(*ffn_in.shape) + halves_of(*ffn_out.shape))(ffn_in, ffn_out)
    order = functools.partial(order_kernel, bits)
    whole_out = call(order, halves_of(n * heads_width, model))(out_weight, rest)
    state = call(
        functools.partial(attend_kernel, merge=False), [shape(rows, heads_width)] * 3, limit=16
    )(queries, *first)
    mixed = call(
        functools.partial(attend_kernel, merge=True), shape(rows, heads_width), limit=16
    )(queries, *state, *later)
    mixes = spread_out(mixed, "head")
    partial = call(functools.partial(post_kernel, n), [block] * n, limit=16)(
        *mixes, *emb, *whole_out, norm1_gain[None, :], norm1_bias[None, :], *ffn
    )
    got = hand_out(partial, "head")
    flipped, stats = call(functools.partial(stats_kernel, n), [shape(width, rows), shape(2, rows)])(*got)
    return call(functools.partial(final_kernel, n), shape(width, rows))(
        flipped, *spread_out(stats, "head"), norm2_gain.reshape(n, 1, width), norm2_bias.reshape(n, 1, width)
    )


def solution(mesh):
    return jax.shard_map(
        on_device,
        mesh=mesh,
        in_specs=(
            P("var", "head"), P("head", None), P(), P(None, "head"), P(None, "head"), P(None, "head"),
            P("head", None), P(), P(), P(None, "head"), P("head", None), P(), P(),
        ),
        out_specs=P("head", "var"),
        check_vma=False,
    )
```

```python
import functools
import math

import jax
import jax.numpy as jnp
from jax import lax
from jax.experimental import pallas as pl
from jax.experimental.pallas import tpu as pltpu
from jax.sharding import PartitionSpec as P


DH = 64
EPS = 1e-05
F32 = jnp.float32
BF16 = jnp.bfloat16
MIB = 1 << 20


def split(x):
    hi = x.astype(BF16)
    return hi, (x - hi.astype(F32)).astype(BF16)


def mm(a, b, dims):
    return lax.dot_general(a, b, (dims, ((), ())), preferred_element_type=F32)


def dot3_split(a, b_hi, b_lo, dims=((1,), (0,))):
    a_hi, a_lo = split(a)
    rows = a.shape[0]
    first = mm(jnp.concatenate([a_hi, a_lo], 0), b_hi, dims)
    return first[:rows] + (first[rows:] + mm(a_hi, b_lo, dims))


def dot3(a, b, dims=((1,), (0,))):
    return dot3_split(a, *split(b), dims)


def butterfly(blocks, pos):
    count = len(blocks)
    out = list(blocks)
    bit = 1
    while bit < count:
        take = (pos & bit) != 0
        out = [jnp.where(take, out[j ^ bit], out[j]) for j in range(count)]
        bit *= 2
    return out


def columns(x, count):
    width = x.shape[1] // count
    return [x[:, j * width : (j + 1) * width] for j in range(count)]


def call(body, outs, scratch=(), limit=12, grid=None, in_specs=None, out_specs=None, flops=0, nbytes=0):
    kwargs = {}
    if grid is not None:
        kwargs = dict(grid=grid, in_specs=in_specs, out_specs=out_specs)
    return pl.pallas_call(
        body,
        out_shape=outs,
        scratch_shapes=list(scratch),
        compiler_params=pltpu.CompilerParams(vmem_limit_bytes=limit * MIB),
        cost_estimate=pl.CostEstimate(flops=flops, bytes_accessed=nbytes, transcendentals=0),
        **kwargs,
    )


def shape(*dims, dtype=F32):
    return jax.ShapeDtypeStruct(dims, dtype)


def halves_of(*dims):
    return [shape(*dims, dtype=BF16)] * 2


def embed_kernel(count, x_hbm, w_hbm, *rest):
    outs, (x_buf, w_buf, x_sems, w_sems) = rest[:count], rest[count:]
    pos = lax.axis_index("head")
    steps, step = w_buf.shape[0], w_buf.shape[1]
    halves, wide = x_buf.shape[0], x_buf.shape[2]
    x_copies = [
        pltpu.make_async_copy(x_hbm.at[:, pl.ds(at * wide, wide)], x_buf.at[at], x_sems.at[at]) for at in range(halves)
    ]
    w_copies = [
        pltpu.make_async_copy(w_hbm.at[pl.ds(at * step, step), :], w_buf.at[at], w_sems.at[at]) for at in range(steps)
    ]
    for at in range(steps):
        if (at * step) % wide == 0:
            x_copies[at * step // wide].start()
        w_copies[at].start()
    total = None
    for at in range(steps):
        half, start = divmod(at * step, wide)
        if start == 0:
            x_copies[half].wait()
        w_copies[at].wait()
        part = dot3(x_buf[half, :, start : start + step], w_buf[at])
        total = part if total is None else total + part
    for ref, block in zip(outs, butterfly(columns(total, count), pos)):
        ref[...] = block


def embed(count, series, emb_weight):
    rows, depth = series.shape
    model = emb_weight.shape[1]
    step = math.gcd(depth, 512)
    steps = depth // step
    halves = 2 if steps % 2 == 0 else 1
    hbm = pl.BlockSpec(memory_space=pltpu.HBM)
    return pl.pallas_call(
        functools.partial(embed_kernel, count),
        out_shape=[shape(rows, model // count)] * count,
        in_specs=[hbm, hbm],
        scratch_shapes=[
            pltpu.VMEM((halves, rows, depth // halves), F32),
            pltpu.VMEM((steps, step, model), F32),
            pltpu.SemaphoreType.DMA((halves,)),
            pltpu.SemaphoreType.DMA((steps,)),
        ],
        name="embed",
        compiler_params=pltpu.CompilerParams(vmem_limit_bytes=126 * MIB // 2),
        cost_estimate=pl.CostEstimate(
            flops=6 * rows * depth * model, bytes_accessed=4 * depth * (model + rows), transcendentals=0
        ),
    )(series, emb_weight)


def piece_of(index, bits):
    return sum(((index >> bit) & 1) << at for at, bit in enumerate(bits))


def cut_kernel(bits, w_ref, out):
    part = piece_of(lax.axis_index("var"), bits)
    size = out.shape[0]
    out[...] = w_ref[pl.ds(pl.multiple_of(part * size, size), size), :]


def order_kernel(bits, own_ref, rest_ref, hi, lo):
    me = piece_of(lax.axis_index("var"), bits)
    rows = own_ref.shape[0]
    size = rows >> len(bits)
    hi[0:rows, :], lo[0:rows, :] = split(own_ref[...])
    for apart in range(1 << len(bits)):
        for k in range(rest_ref.shape[1]):
            at = pl.ds(pl.multiple_of((k + 1) * rows + (me ^ apart) * size, size), size)
            hi[at, :], lo[at, :] = split(rest_ref[apart, k])


def bias_kernel(x_ref, bias, out):
    out[...] = x_ref[...] + bias[lax.axis_index("head")]


def add_kernel(*refs):
    total = refs[0][...]
    for part in refs[1:-1]:
        total = total + part[...]
    refs[-1][...] = total


def split_kernel(*refs):
    count = len(refs) // 3
    for at in range(count):
        refs[count + 2 * at][...], refs[count + 2 * at + 1][...] = split(refs[at][...])


def ordered_kernel(count, k_ref, v_ref, q_ref, *outs):
    pos = lax.axis_index("head")
    width, cols = k_ref.shape[0] // count, k_ref.shape[1]
    for k in range(count):
        rows = pl.ds(pl.multiple_of((pos ^ k) * width, width), width)
        at = slice(k * width, (k + 1) * width)
        outs[0][at, :cols], outs[1][at, :cols] = split(k_ref[rows, :])
        outs[0][at, cols:], outs[1][at, cols:] = split(v_ref[rows, :])
        outs[2][at, :], outs[3][at, :] = split(q_ref[rows, :] * (1.0 / math.sqrt(DH)))


def project_kernel(*refs):
    blocks, hi, lo, out = refs[:-3], *refs[-3:]
    out[...] = dot3_split(jnp.concatenate([block[...] for block in blocks], 1), hi[...], lo[...])


def by_head(stacked, heads):
    rows = stacked.shape[0] // heads
    lane = lax.broadcasted_iota(jnp.int32, (rows, stacked.shape[1]), 1) // DH
    out = stacked[:rows]
    for head in range(1, heads):
        out = jnp.where(lane == head, stacked[head * rows : (head + 1) * rows], out)
    return out


def attend_kernel(q_ref, *refs, merge):
    if merge:
        (acc_a, top_a, sum_a), pieces, out = refs[:3], refs[3:-1], refs[-1]
    else:
        pieces, (acc_out, top_out, sum_out) = refs[:-3], refs[-3:]
    rows, wide = q_ref.shape
    heads = wide // DH
    query = q_ref[...]
    lane = lax.broadcasted_iota(jnp.int32, query.shape, 1) // DH
    stacked = jnp.concatenate([jnp.where(lane == head, query, 0.0) for head in range(heads)], 0)
    keys = jnp.concatenate([piece[:, :wide] for piece in pieces], 0)
    v_hi, v_lo = split(jnp.concatenate([piece[:, wide:] for piece in pieces], 0))
    scores = dot3(stacked, keys, ((1,), (1,)))
    top = jnp.max(scores, axis=1, keepdims=True)
    w_hi, w_lo = split(jnp.exp(scores - top))
    along = ((1,), (0,))
    both = mm(jnp.concatenate([w_hi, w_lo], 0), jnp.concatenate([v_hi, jnp.ones_like(v_hi)], 1), along)
    both = both[: heads * rows] + both[heads * rows :]
    acc = by_head(both[:, :wide] + mm(w_hi, v_lo, along), heads)
    total = by_head(both[:, wide:], heads)
    top = by_head(jnp.broadcast_to(top, (heads * rows, wide)), heads)
    if merge:
        high = jnp.maximum(top, top_a[...])
        fade_a, fade = jnp.exp(top_a[...] - high), jnp.exp(top - high)
        out[...] = (acc * fade + acc_a[...] * fade_a) / (total * fade + sum_a[...] * fade_a)
    else:
        acc_out[...] = acc
        top_out[...] = top
        sum_out[...] = total


def normalise(x, gain, bias):
    centre = jnp.mean(x, axis=-1, keepdims=True)
    spread = x - centre
    variance = jnp.mean(spread * spread, axis=-1, keepdims=True)
    return spread * lax.rsqrt(variance + EPS) * gain + bias


def gelu(v):
    return 0.5 * v * (1.0 + lax.erf(v * (1.0 / math.sqrt(2.0))))


def post_kernel(count, *refs):
    pos = lax.axis_index("head")
    mixed, emb = refs[:count], refs[count : 2 * count]
    o_hi, o_lo, gain, bias, in_hi, in_lo, out_hi, out_lo = refs[2 * count : 2 * count + 8]
    outs = refs[2 * count + 8 :]
    stream = jnp.concatenate([m[...] for m in mixed], 1)
    attention = dot3_split(stream, o_hi[...], o_lo[...])
    embedded = jnp.concatenate(butterfly([e[...] for e in emb], pos), 1)
    normed = normalise(embedded + attention, gain[...], bias[...])
    hidden = gelu(dot3_split(normed, in_hi[...], in_lo[...]))
    partial = butterfly(columns(dot3_split(hidden, out_hi[...], out_lo[...]), count), pos)
    mine = butterfly(columns(normed, count), pos)[0]
    outs[0][...] = mine + partial[0]
    for ref, block in zip(outs[1:], partial[1:]):
        ref[...] = block


def stats_kernel(count, *refs):
    parts, out, stats = refs[:count], refs[count], refs[count + 1]
    total = parts[0][...]
    for part in parts[1:]:
        total = total + part[...]
    flipped = total.T
    centre = jnp.mean(flipped, axis=0, keepdims=True)
    spread = flipped - centre
    out[...] = flipped
    stats[...] = jnp.concatenate([centre, jnp.sum(spread * spread, axis=0, keepdims=True)], 0)


def final_kernel(count, x_ref, *refs):
    pos = lax.axis_index("head")
    stats, gain, bias, out = refs[:count], refs[count], refs[count + 1], refs[count + 2]
    width = x_ref.shape[0]
    centres = [s[0:1, :] for s in stats]
    centre = sum(centres[1:], centres[0]) * (1.0 / count)
    square = sum((s[1:2, :] for s in stats[1:]), stats[0][1:2, :])
    for each in centres:
        square = square + width * (each - centre) * (each - centre)
    scale = lax.rsqrt(square * (1.0 / (count * width)) + EPS)
    pair = jnp.concatenate([gain[pos], bias[pos], jnp.zeros((6, width), F32)], 0).T
    out[...] = (x_ref[...] - centre) * scale * pair[:, 0:1] + pair[:, 1:2]


def send(x, axis, offset):
    size = lax.axis_size(axis)
    return lax.ppermute(x, axis, [(i, i ^ offset) for i in range(size)])


def spread_out(x, axis):
    return [x] + [send(x, axis, k) for k in range(1, lax.axis_size(axis))]


def hand_out(parts, axis):
    return [parts[0]] + [send(parts[k], axis, k) for k in range(1, lax.axis_size(axis))]


def bits_below(count):
    return [1 << at for at in range(count.bit_length() - 1)]


def gather_pieces(piece):
    size = lax.axis_size("var")
    if size != 8:
        whole = lax.all_gather(piece, "var", axis=0, tiled=True)
        cut = whole.shape[0] // 2
        return [whole[:cut]], [whole[cut:]]

    def hop(x, even, odd):
        return lax.ppermute(x, "var", [(i, i ^ (odd if i & 1 else even)) for i in range(size)])

    got_a = hop(piece, 4, 2)
    got_b = hop(piece, 2, 4)
    got_ab = hop(got_a, 2, 4)
    swap, swap_a, swap_b, swap_ab = (
        hop(each, 1, 1) for each in (piece, got_a, got_b, got_ab)
    )
    return [piece, got_a, got_b, swap], [swap_a, swap_b, got_ab, swap_ab]


def on_device(
    series, emb_weight, emb_bias, q_weight, k_weight, v_weight, out_weight,
    norm1_gain, norm1_bias, ffn_in, ffn_out, norm2_gain, norm2_bias,
):
    n = lax.axis_size("head")
    rows, _ = series.shape
    model = emb_weight.shape[1]
    width = model // n
    heads_width = q_weight.shape[1]
    block = shape(rows, width)

    var_bits = lax.axis_size("var").bit_length() - 1
    bits = [var_bits - 1, 0]
    parts = embed(n, series, emb_weight)
    got = hand_out(parts, "head")
    got[0] = call(bias_kernel, block)(parts[0], emb_bias.reshape(n, 1, width))
    cut = call(functools.partial(cut_kernel, bits), shape(heads_width >> len(bits), model))(out_weight)
    have = cut[None]
    for bit in bits_below(n):
        have = jnp.concatenate([have, send(have, "head", bit)], 0)
    rest = have[None, 1:]
    mine = call(add_kernel, block)(*got)
    emb = spread_out(mine, "head")
    for bit in bits:
        rest = jnp.concatenate([rest, send(rest, "var", 1 << bit)], 0)
    wide = halves_of(model, 2 * heads_width) + halves_of(model, heads_width)
    kv_hi, kv_lo, q_hi, q_lo = call(functools.partial(ordered_kernel, n), wide)(k_weight, v_weight, q_weight)
    pair = call(project_kernel, shape(rows, 2 * heads_width))(*emb, kv_hi, kv_lo)
    queries = call(project_kernel, shape(rows, heads_width))(*emb, q_hi, q_lo)
    first, later = gather_pieces(pair)
    ffn = call(split_kernel, halves_of(*ffn_in.shape) + halves_of(*ffn_out.shape))(ffn_in, ffn_out)
    order = functools.partial(order_kernel, bits)
    whole_out = call(order, halves_of(n * heads_width, model))(out_weight, rest)
    state = call(
        functools.partial(attend_kernel, merge=False), [shape(rows, heads_width)] * 3, limit=16
    )(queries, *first)
    mixed = call(
        functools.partial(attend_kernel, merge=True), shape(rows, heads_width), limit=16
    )(queries, *state, *later)
    mixes = spread_out(mixed, "head")
    partial = call(functools.partial(post_kernel, n), [block] * n, limit=16)(
        *mixes, *emb, *whole_out, norm1_gain[None, :], norm1_bias[None, :], *ffn
    )
    got = hand_out(partial, "head")
    flipped, stats = call(functools.partial(stats_kernel, n), [shape(width, rows), shape(2, rows)])(*got)
    return call(functools.partial(final_kernel, n), shape(width, rows))(
        flipped, *spread_out(stats, "head"), norm2_gain.reshape(n, 1, width), norm2_bias.reshape(n, 1, width)
    )


def solution(mesh):
    return jax.shard_map(
        on_device,
        mesh=mesh,
        in_specs=(
            P("var", "head"), P("head", None), P(), P(None, "head"), P(None, "head"), P(None, "head"),
            P("head", None), P(), P(), P(None, "head"), P("head", None), P(), P(),
        ),
        out_specs=P("head", "var"),
        check_vma=False,
    )
```

```python
import functools
import math

import jax
import jax.numpy as jnp
from jax import lax
from jax.experimental import pallas as pl
from jax.experimental.pallas import tpu as pltpu
from jax.sharding import PartitionSpec as P


DH = 64
EPS = 1e-05
F32 = jnp.float32
BF16 = jnp.bfloat16
MIB = 1 << 20


def split(x):
    hi = x.astype(BF16)
    return hi, (x - hi.astype(F32)).astype(BF16)


def mm(a, b, dims):
    return lax.dot_general(a, b, (dims, ((), ())), preferred_element_type=F32)


def dot3_split(a, b_hi, b_lo, dims=((1,), (0,))):
    a_hi, a_lo = split(a)
    rows = a.shape[0]
    first = mm(jnp.concatenate([a_hi, a_lo], 0), b_hi, dims)
    return first[:rows] + (first[rows:] + mm(a_hi, b_lo, dims))


def dot3(a, b, dims=((1,), (0,))):
    return dot3_split(a, *split(b), dims)


def butterfly(blocks, pos):
    count = len(blocks)
    out = list(blocks)
    bit = 1
    while bit < count:
        take = (pos & bit) != 0
        out = [jnp.where(take, out[j ^ bit], out[j]) for j in range(count)]
        bit *= 2
    return out


def columns(x, count):
    width = x.shape[1] // count
    return [x[:, j * width : (j + 1) * width] for j in range(count)]


def call(body, outs, scratch=(), limit=12, grid=None, in_specs=None, out_specs=None, flops=0, nbytes=0):
    kwargs = {}
    if grid is not None:
        kwargs = dict(grid=grid, in_specs=in_specs, out_specs=out_specs)
    return pl.pallas_call(
        body,
        out_shape=outs,
        scratch_shapes=list(scratch),
        compiler_params=pltpu.CompilerParams(vmem_limit_bytes=limit * MIB),
        cost_estimate=pl.CostEstimate(flops=flops, bytes_accessed=nbytes, transcendentals=0),
        **kwargs,
    )


def shape(*dims, dtype=F32):
    return jax.ShapeDtypeStruct(dims, dtype)


def halves_of(*dims):
    return [shape(*dims, dtype=BF16)] * 2


def embed_kernel(count, x_hbm, w_hbm, *rest):
    outs, (x_buf, w_buf, x_sems, w_sems) = rest[:count], rest[count:]
    pos = lax.axis_index("head")
    steps, step = w_buf.shape[0], w_buf.shape[1]
    halves, wide = x_buf.shape[0], x_buf.shape[2]
    x_copies = [
        pltpu.make_async_copy(x_hbm.at[:, pl.ds(at * wide, wide)], x_buf.at[at], x_sems.at[at]) for at in range(halves)
    ]
    w_copies = [
        pltpu.make_async_copy(w_hbm.at[pl.ds(at * step, step), :], w_buf.at[at], w_sems.at[at]) for at in range(steps)
    ]
    for at in range(steps):
        if (at * step) % wide == 0:
            x_copies[at * step // wide].start()
        w_copies[at].start()
    total = None
    for at in range(steps):
        half, start = divmod(at * step, wide)
        if start == 0:
            x_copies[half].wait()
        w_copies[at].wait()
        part = dot3(x_buf[half, :, start : start + step], w_buf[at])
        total = part if total is None else total + part
    for ref, block in zip(outs, butterfly(columns(total, count), pos)):
        ref[...] = block


def embed(count, series, emb_weight):
    rows, depth = series.shape
    model = emb_weight.shape[1]
    step = math.gcd(depth, 512)
    steps = depth // step
    halves = 2 if steps % 2 == 0 else 1
    hbm = pl.BlockSpec(memory_space=pltpu.HBM)
    return pl.pallas_call(
        functools.partial(embed_kernel, count),
        out_shape=[shape(rows, model // count)] * count,
        in_specs=[hbm, hbm],
        scratch_shapes=[
            pltpu.VMEM((halves, rows, depth // halves), F32),
            pltpu.VMEM((steps, step, model), F32),
            pltpu.SemaphoreType.DMA((halves,)),
            pltpu.SemaphoreType.DMA((steps,)),
        ],
        name="embed",
        compiler_params=pltpu.CompilerParams(vmem_limit_bytes=126 * MIB // 2),
        cost_estimate=pl.CostEstimate(
            flops=6 * rows * depth * model, bytes_accessed=4 * depth * (model + rows), transcendentals=0
        ),
    )(series, emb_weight)


def piece_of(index, bits):
    return sum(((index >> bit) & 1) << at for at, bit in enumerate(bits))


def cut_kernel(bits, w_ref, out):
    part = piece_of(lax.axis_index("var"), bits)
    size = out.shape[0]
    out[...] = w_ref[pl.ds(pl.multiple_of(part * size, size), size), :]


def order_kernel(bits, own_ref, rest_ref, hi, lo):
    me = piece_of(lax.axis_index("var"), bits)
    rows = own_ref.shape[0]
    size = rows >> len(bits)
    hi[0:rows, :], lo[0:rows, :] = split(own_ref[...])
    for apart in range(1 << len(bits)):
        for k in range(rest_ref.shape[1]):
            at = pl.ds(pl.multiple_of((k + 1) * rows + (me ^ apart) * size, size), size)
            hi[at, :], lo[at, :] = split(rest_ref[apart, k])


def bias_kernel(x_ref, bias, out):
    out[...] = x_ref[...] + bias[lax.axis_index("head")]


def add_kernel(*refs):
    total = refs[0][...]
    for part in refs[1:-1]:
        total = total + part[...]
    refs[-1][...] = total


def split_kernel(*refs):
    count = len(refs) // 3
    for at in range(count):
        refs[count + 2 * at][...], refs[count + 2 * at + 1][...] = split(refs[at][...])


def ordered_kernel(count, k_ref, v_ref, q_ref, *outs):
    pos = lax.axis_index("head")
    width, cols = k_ref.shape[0] // count, k_ref.shape[1]
    for k in range(count):
        rows = pl.ds(pl.multiple_of((pos ^ k) * width, width), width)
        at = slice(k * width, (k + 1) * width)
        outs[0][at, :cols], outs[1][at, :cols] = split(k_ref[rows, :])
        outs[0][at, cols:], outs[1][at, cols:] = split(v_ref[rows, :])
        outs[2][at, :], outs[3][at, :] = split(q_ref[rows, :] * (1.0 / math.sqrt(DH)))


def project_kernel(*refs):
    blocks, hi, lo, out = refs[:-3], *refs[-3:]
    out[...] = dot3_split(jnp.concatenate([block[...] for block in blocks], 1), hi[...], lo[...])


def by_head(stacked, heads):
    rows = stacked.shape[0] // heads
    lane = lax.broadcasted_iota(jnp.int32, (rows, stacked.shape[1]), 1) // DH
    out = stacked[:rows]
    for head in range(1, heads):
        out = jnp.where(lane == head, stacked[head * rows : (head + 1) * rows], out)
    return out


def attend_kernel(q_ref, *refs, merge):
    if merge:
        (acc_a, top_a, sum_a), pieces, out = refs[:3], refs[3:-1], refs[-1]
    else:
        pieces, (acc_out, top_out, sum_out) = refs[:-3], refs[-3:]
    rows, wide = q_ref.shape
    heads = wide // DH
    query = q_ref[...]
    lane = lax.broadcasted_iota(jnp.int32, query.shape, 1) // DH
    stacked = jnp.concatenate([jnp.where(lane == head, query, 0.0) for head in range(heads)], 0)
    keys = jnp.concatenate([piece[:, :wide] for piece in pieces], 0)
    v_hi, v_lo = split(jnp.concatenate([piece[:, wide:] for piece in pieces], 0))
    scores = dot3(stacked, keys, ((1,), (1,)))
    top = jnp.max(scores, axis=1, keepdims=True)
    w_hi, w_lo = split(jnp.exp(scores - top))
    along = ((1,), (0,))
    both = mm(jnp.concatenate([w_hi, w_lo], 0), jnp.concatenate([v_hi, jnp.ones_like(v_hi)], 1), along)
    both = both[: heads * rows] + both[heads * rows :]
    acc = by_head(both[:, :wide] + mm(w_hi, v_lo, along), heads)
    total = by_head(both[:, wide:], heads)
    top = by_head(jnp.broadcast_to(top, (heads * rows, wide)), heads)
    if merge:
        high = jnp.maximum(top, top_a[...])
        fade_a, fade = jnp.exp(top_a[...] - high), jnp.exp(top - high)
        out[...] = (acc * fade + acc_a[...] * fade_a) / (total * fade + sum_a[...] * fade_a)
    else:
        acc_out[...] = acc
        top_out[...] = top
        sum_out[...] = total


def normalise(x, gain, bias):
    centre = jnp.mean(x, axis=-1, keepdims=True)
    spread = x - centre
    variance = jnp.mean(spread * spread, axis=-1, keepdims=True)
    return spread * lax.rsqrt(variance + EPS) * gain + bias


def gelu(v):
    return 0.5 * v * (1.0 + lax.erf(v * (1.0 / math.sqrt(2.0))))


def post_kernel(count, *refs):
    pos = lax.axis_index("head")
    mixed, emb = refs[:count], refs[count : 2 * count]
    o_hi, o_lo, gain, bias, in_hi, in_lo, out_hi, out_lo = refs[2 * count : 2 * count + 8]
    outs = refs[2 * count + 8 :]
    stream = jnp.concatenate([m[...] for m in mixed], 1)
    attention = dot3_split(stream, o_hi[...], o_lo[...])
    embedded = jnp.concatenate(butterfly([e[...] for e in emb], pos), 1)
    normed = normalise(embedded + attention, gain[...], bias[...])
    hidden = gelu(dot3_split(normed, in_hi[...], in_lo[...]))
    partial = butterfly(columns(dot3_split(hidden, out_hi[...], out_lo[...]), count), pos)
    mine = butterfly(columns(normed, count), pos)[0]
    outs[0][...] = mine + partial[0]
    for ref, block in zip(outs[1:], partial[1:]):
        ref[...] = block


def stats_kernel(count, *refs):
    parts, out, stats = refs[:count], refs[count], refs[count + 1]
    total = parts[0][...]
    for part in parts[1:]:
        total = total + part[...]
    flipped = total.T
    centre = jnp.mean(flipped, axis=0, keepdims=True)
    spread = flipped - centre
    out[...] = flipped
    stats[...] = jnp.concatenate([centre, jnp.sum(spread * spread, axis=0, keepdims=True)], 0)


def final_kernel(count, x_ref, *refs):
    pos = lax.axis_index("head")
    stats, gain, bias, out = refs[:count], refs[count], refs[count + 1], refs[count + 2]
    width = x_ref.shape[0]
    centres = [s[0:1, :] for s in stats]
    centre = sum(centres[1:], centres[0]) * (1.0 / count)
    square = sum((s[1:2, :] for s in stats[1:]), stats[0][1:2, :])
    for each in centres:
        square = square + width * (each - centre) * (each - centre)
    scale = lax.rsqrt(square * (1.0 / (count * width)) + EPS)
    pair = jnp.concatenate([gain[pos], bias[pos], jnp.zeros((6, width), F32)], 0).T
    out[...] = (x_ref[...] - centre) * scale * pair[:, 0:1] + pair[:, 1:2]


def send(x, axis, offset):
    size = lax.axis_size(axis)
    return lax.ppermute(x, axis, [(i, i ^ offset) for i in range(size)])


def spread_out(x, axis):
    return [x] + [send(x, axis, k) for k in range(1, lax.axis_size(axis))]


def hand_out(parts, axis):
    return [parts[0]] + [send(parts[k], axis, k) for k in range(1, lax.axis_size(axis))]


def bits_below(count):
    return [1 << at for at in range(count.bit_length() - 1)]


def gather_pieces(piece):
    size = lax.axis_size("var")
    if size > 8:
        whole = lax.all_gather(piece, "var", axis=0, tiled=True)
        cut = whole.shape[0] // 2
        return [whole[:cut]], [whole[cut:]]
    far = [piece] + [send(piece, "var", k) for k in range(2, size, 2)]
    near = [send(each, "var", 1) for each in far]
    return far + near[:1], near[1:]


def on_device(
    series, emb_weight, emb_bias, q_weight, k_weight, v_weight, out_weight,
    norm1_gain, norm1_bias, ffn_in, ffn_out, norm2_gain, norm2_bias,
):
    n = lax.axis_size("head")
    rows, _ = series.shape
    model = emb_weight.shape[1]
    width = model // n
    heads_width = q_weight.shape[1]
    block = shape(rows, width)

    var_bits = lax.axis_size("var").bit_length() - 1
    bits = [var_bits - 1, 0]
    parts = embed(n, series, emb_weight)
    got = hand_out(parts, "head")
    got[0] = call(bias_kernel, block)(parts[0], emb_bias.reshape(n, 1, width))
    cut = call(functools.partial(cut_kernel, bits), shape(heads_width >> len(bits), model))(out_weight)
    have = cut[None]
    for bit in bits_below(n):
        have = jnp.concatenate([have, send(have, "head", bit)], 0)
    rest = have[None, 1:]
    mine = call(add_kernel, block)(*got)
    emb = spread_out(mine, "head")
    for bit in bits:
        rest = jnp.concatenate([rest, send(rest, "var", 1 << bit)], 0)
    wide = halves_of(model, 2 * heads_width) + halves_of(model, heads_width)
    kv_hi, kv_lo, q_hi, q_lo = call(functools.partial(ordered_kernel, n), wide)(k_weight, v_weight, q_weight)
    pair = call(project_kernel, shape(rows, 2 * heads_width))(*emb, kv_hi, kv_lo)
    queries = call(project_kernel, shape(rows, heads_width))(*emb, q_hi, q_lo)
    first, later = gather_pieces(pair)
    ffn = call(split_kernel, halves_of(*ffn_in.shape) + halves_of(*ffn_out.shape))(ffn_in, ffn_out)
    order = functools.partial(order_kernel, bits)
    whole_out = call(order, halves_of(n * heads_width, model))(out_weight, rest)
    state = call(
        functools.partial(attend_kernel, merge=False), [shape(rows, heads_width)] * 3, limit=16
    )(queries, *first)
    mixed = call(
        functools.partial(attend_kernel, merge=True), shape(rows, heads_width), limit=16
    )(queries, *state, *later)
    mixes = spread_out(mixed, "head")
    partial = call(functools.partial(post_kernel, n), [block] * n, limit=16)(
        *mixes, *emb, *whole_out, norm1_gain[None, :], norm1_bias[None, :], *ffn
    )
    got = hand_out(partial, "head")
    flipped, stats = call(functools.partial(stats_kernel, n), [shape(width, rows), shape(2, rows)])(*got)
    return call(functools.partial(final_kernel, n), shape(width, rows))(
        flipped, *spread_out(stats, "head"), norm2_gain.reshape(n, 1, width), norm2_bias.reshape(n, 1, width)
    )


def solution(mesh):
    return jax.shard_map(
        on_device,
        mesh=mesh,
        in_specs=(
            P("var", "head"), P("head", None), P(), P(None, "head"), P(None, "head"), P(None, "head"),
            P("head", None), P(), P(), P(None, "head"), P("head", None), P(), P(),
        ),
        out_specs=P("head", "var"),
        check_vma=False,
    )
```

```python
import functools
import math

import jax
import jax.numpy as jnp
from jax import lax
from jax.experimental import pallas as pl
from jax.experimental.pallas import tpu as pltpu
from jax.sharding import PartitionSpec as P


DH = 64
EPS = 1e-05
F32 = jnp.float32
BF16 = jnp.bfloat16
MIB = 1 << 20


def split(x):
    hi = x.astype(BF16)
    return hi, (x - hi.astype(F32)).astype(BF16)


def mm(a, b, dims):
    return lax.dot_general(a, b, (dims, ((), ())), preferred_element_type=F32)


def dot3_split(a, b_hi, b_lo, dims=((1,), (0,))):
    a_hi, a_lo = split(a)
    rows = a.shape[0]
    first = mm(jnp.concatenate([a_hi, a_lo], 0), b_hi, dims)
    return first[:rows] + (first[rows:] + mm(a_hi, b_lo, dims))


def dot3(a, b, dims=((1,), (0,))):
    return dot3_split(a, *split(b), dims)


def butterfly(blocks, pos):
    count = len(blocks)
    out = list(blocks)
    bit = 1
    while bit < count:
        take = (pos & bit) != 0
        out = [jnp.where(take, out[j ^ bit], out[j]) for j in range(count)]
        bit *= 2
    return out


def columns(x, count):
    width = x.shape[1] // count
    return [x[:, j * width : (j + 1) * width] for j in range(count)]


def call(body, outs, scratch=(), limit=12, grid=None, in_specs=None, out_specs=None, flops=0, nbytes=0):
    kwargs = {}
    if grid is not None:
        kwargs = dict(grid=grid, in_specs=in_specs, out_specs=out_specs)
    return pl.pallas_call(
        body,
        out_shape=outs,
        scratch_shapes=list(scratch),
        compiler_params=pltpu.CompilerParams(vmem_limit_bytes=limit * MIB),
        cost_estimate=pl.CostEstimate(flops=flops, bytes_accessed=nbytes, transcendentals=0),
        **kwargs,
    )


def shape(*dims, dtype=F32):
    return jax.ShapeDtypeStruct(dims, dtype)


def halves_of(*dims):
    return [shape(*dims, dtype=BF16)] * 2


def embed_kernel(count, x_hbm, w_hbm, *rest):
    outs, (x_buf, w_buf, x_sems, w_sems) = rest[:count], rest[count:]
    pos = lax.axis_index("head")
    steps, step = w_buf.shape[0], w_buf.shape[1]
    halves, wide = x_buf.shape[0], x_buf.shape[2]
    x_copies = [
        pltpu.make_async_copy(x_hbm.at[:, pl.ds(at * wide, wide)], x_buf.at[at], x_sems.at[at]) for at in range(halves)
    ]
    w_copies = [
        pltpu.make_async_copy(w_hbm.at[pl.ds(at * step, step), :], w_buf.at[at], w_sems.at[at]) for at in range(steps)
    ]
    for at in range(steps):
        if (at * step) % wide == 0:
            x_copies[at * step // wide].start()
        w_copies[at].start()
    total = None
    for at in range(steps):
        half, start = divmod(at * step, wide)
        if start == 0:
            x_copies[half].wait()
        w_copies[at].wait()
        part = dot3(x_buf[half, :, start : start + step], w_buf[at])
        total = part if total is None else total + part
    for ref, block in zip(outs, butterfly(columns(total, count), pos)):
        ref[...] = block


def embed(count, series, emb_weight):
    rows, depth = series.shape
    model = emb_weight.shape[1]
    step = math.gcd(depth, 512)
    steps = depth // step
    halves = 2 if steps % 2 == 0 else 1
    hbm = pl.BlockSpec(memory_space=pltpu.HBM)
    return pl.pallas_call(
        functools.partial(embed_kernel, count),
        out_shape=[shape(rows, model // count)] * count,
        in_specs=[hbm, hbm],
        scratch_shapes=[
            pltpu.VMEM((halves, rows, depth // halves), F32),
            pltpu.VMEM((steps, step, model), F32),
            pltpu.SemaphoreType.DMA((halves,)),
            pltpu.SemaphoreType.DMA((steps,)),
        ],
        name="embed",
        compiler_params=pltpu.CompilerParams(vmem_limit_bytes=126 * MIB // 2),
        cost_estimate=pl.CostEstimate(
            flops=6 * rows * depth * model, bytes_accessed=4 * depth * (model + rows), transcendentals=0
        ),
    )(series, emb_weight)


def piece_of(index, bits):
    return sum(((index >> bit) & 1) << at for at, bit in enumerate(bits))


def cut_kernel(bits, w_ref, out):
    part = piece_of(lax.axis_index("var"), bits)
    size = out.shape[0]
    out[...] = w_ref[pl.ds(pl.multiple_of(part * size, size), size), :]


def order_kernel(bits, own_ref, rest_ref, hi, lo):
    me = piece_of(lax.axis_index("var"), bits)
    rows = own_ref.shape[0]
    size = rows >> len(bits)
    hi[0:rows, :], lo[0:rows, :] = split(own_ref[...])
    for apart in range(1 << len(bits)):
        for k in range(rest_ref.shape[1]):
            at = pl.ds(pl.multiple_of((k + 1) * rows + (me ^ apart) * size, size), size)
            hi[at, :], lo[at, :] = split(rest_ref[apart, k])


def bias_kernel(x_ref, bias, out):
    out[...] = x_ref[...] + bias[lax.axis_index("head")]


def add_kernel(*refs):
    total = refs[0][...]
    for part in refs[1:-1]:
        total = total + part[...]
    refs[-1][...] = total


def split_kernel(*refs):
    count = len(refs) // 3
    for at in range(count):
        refs[count + 2 * at][...], refs[count + 2 * at + 1][...] = split(refs[at][...])


def ordered_kernel(count, k_ref, v_ref, q_ref, *outs):
    pos = lax.axis_index("head")
    width, cols = k_ref.shape[0] // count, k_ref.shape[1]
    for k in range(count):
        rows = pl.ds(pl.multiple_of((pos ^ k) * width, width), width)
        at = slice(k * width, (k + 1) * width)
        outs[0][at, :cols], outs[1][at, :cols] = split(k_ref[rows, :])
        outs[0][at, cols:], outs[1][at, cols:] = split(v_ref[rows, :])
        outs[2][at, :], outs[3][at, :] = split(q_ref[rows, :] * (1.0 / math.sqrt(DH)))


def project_kernel(*refs):
    blocks, hi, lo, out = refs[:-3], *refs[-3:]
    out[...] = dot3_split(jnp.concatenate([block[...] for block in blocks], 1), hi[...], lo[...])


def by_head(stacked, heads):
    rows = stacked.shape[0] // heads
    lane = lax.broadcasted_iota(jnp.int32, (rows, stacked.shape[1]), 1) // DH
    out = stacked[:rows]
    for head in range(1, heads):
        out = jnp.where(lane == head, stacked[head * rows : (head + 1) * rows], out)
    return out


def attend_kernel(q_ref, *refs, merge):
    if merge:
        (acc_a, top_a, sum_a), pieces, out = refs[:3], refs[3:-1], refs[-1]
    else:
        pieces, (acc_out, top_out, sum_out) = refs[:-3], refs[-3:]
    rows, wide = q_ref.shape
    heads = wide // DH
    query = q_ref[...]
    lane = lax.broadcasted_iota(jnp.int32, query.shape, 1) // DH
    stacked = jnp.concatenate([jnp.where(lane == head, query, 0.0) for head in range(heads)], 0)
    k_hi, k_lo = split(jnp.concatenate([piece[:, :wide] for piece in pieces], 0))
    v_hi, v_lo = split(jnp.concatenate([piece[:, wide:] for piece in pieces], 0))
    s_hi, s_lo = split(stacked)
    queries = jnp.concatenate(
        [jnp.concatenate([s_hi, s_hi], 1), jnp.concatenate([s_lo, jnp.zeros_like(s_lo)], 1)], 0
    )
    scores = mm(queries, jnp.concatenate([k_hi, k_lo], 1), ((1,), (1,)))
    scores = scores[: heads * rows] + scores[heads * rows :]
    top = jnp.max(scores, axis=1, keepdims=True)
    weights = jnp.exp(scores - top)
    total = jnp.sum(weights, axis=1, keepdims=True)
    both = mm(jnp.concatenate(split(weights), 0), jnp.concatenate([v_hi, v_lo], 1), ((1,), (0,)))
    above, below = both[: heads * rows], both[heads * rows :]
    acc = by_head(above[:, :wide] + (above[:, wide:] + below[:, :wide]), heads)
    total = by_head(jnp.broadcast_to(total, (heads * rows, wide)), heads)
    top = by_head(jnp.broadcast_to(top, (heads * rows, wide)), heads)
    if merge:
        high = jnp.maximum(top, top_a[...])
        fade_a, fade = jnp.exp(top_a[...] - high), jnp.exp(top - high)
        out[...] = (acc * fade + acc_a[...] * fade_a) / (total * fade + sum_a[...] * fade_a)
    else:
        acc_out[...] = acc
        top_out[...] = top
        sum_out[...] = total


def normalise(x, gain, bias):
    centre = jnp.mean(x, axis=-1, keepdims=True)
    spread = x - centre
    variance = jnp.mean(spread * spread, axis=-1, keepdims=True)
    return spread * lax.rsqrt(variance + EPS) * gain + bias


def gelu(v):
    return 0.5 * v * (1.0 + lax.erf(v * (1.0 / math.sqrt(2.0))))


def post_kernel(count, *refs):
    pos = lax.axis_index("head")
    mixed, emb = refs[:count], refs[count : 2 * count]
    o_hi, o_lo, gain, bias, in_hi, in_lo, out_hi, out_lo = refs[2 * count : 2 * count + 8]
    outs = refs[2 * count + 8 :]
    stream = jnp.concatenate([m[...] for m in mixed], 1)
    attention = dot3_split(stream, o_hi[...], o_lo[...])
    embedded = jnp.concatenate(butterfly([e[...] for e in emb], pos), 1)
    normed = normalise(embedded + attention, gain[...], bias[...])
    hidden = gelu(dot3_split(normed, in_hi[...], in_lo[...]))
    partial = butterfly(columns(dot3_split(hidden, out_hi[...], out_lo[...]), count), pos)
    mine = butterfly(columns(normed, count), pos)[0]
    outs[0][...] = mine + partial[0]
    for ref, block in zip(outs[1:], partial[1:]):
        ref[...] = block


def stats_kernel(count, *refs):
    parts, out, stats = refs[:count], refs[count], refs[count + 1]
    total = parts[0][...]
    for part in parts[1:]:
        total = total + part[...]
    flipped = total.T
    centre = jnp.mean(flipped, axis=0, keepdims=True)
    spread = flipped - centre
    out[...] = flipped
    stats[...] = jnp.concatenate([centre, jnp.sum(spread * spread, axis=0, keepdims=True)], 0)


def final_kernel(count, x_ref, *refs):
    pos = lax.axis_index("head")
    stats, gain, bias, out = refs[:count], refs[count], refs[count + 1], refs[count + 2]
    width = x_ref.shape[0]
    centres = [s[0:1, :] for s in stats]
    centre = sum(centres[1:], centres[0]) * (1.0 / count)
    square = sum((s[1:2, :] for s in stats[1:]), stats[0][1:2, :])
    for each in centres:
        square = square + width * (each - centre) * (each - centre)
    scale = lax.rsqrt(square * (1.0 / (count * width)) + EPS)
    pair = jnp.concatenate([gain[pos], bias[pos], jnp.zeros((6, width), F32)], 0).T
    out[...] = (x_ref[...] - centre) * scale * pair[:, 0:1] + pair[:, 1:2]


def send(x, axis, offset):
    size = lax.axis_size(axis)
    return lax.ppermute(x, axis, [(i, i ^ offset) for i in range(size)])


def spread_out(x, axis):
    return [x] + [send(x, axis, k) for k in range(1, lax.axis_size(axis))]


def hand_out(parts, axis):
    return [parts[0]] + [send(parts[k], axis, k) for k in range(1, lax.axis_size(axis))]


def bits_below(count):
    return [1 << at for at in range(count.bit_length() - 1)]


def gather_pieces(piece):
    size = lax.axis_size("var")
    if size > 8:
        whole = lax.all_gather(piece, "var", axis=0, tiled=True)
        cut = whole.shape[0] // 2
        return [whole[:cut]], [whole[cut:]]
    far = [piece] + [send(piece, "var", k) for k in range(2, size, 2)]
    near = [send(each, "var", 1) for each in far]
    return far[:-1] + near[:-1], [far[-1], near[-1]]


def on_device(
    series, emb_weight, emb_bias, q_weight, k_weight, v_weight, out_weight,
    norm1_gain, norm1_bias, ffn_in, ffn_out, norm2_gain, norm2_bias,
):
    n = lax.axis_size("head")
    rows, _ = series.shape
    model = emb_weight.shape[1]
    width = model // n
    heads_width = q_weight.shape[1]
    block = shape(rows, width)

    var_bits = lax.axis_size("var").bit_length() - 1
    bits = [var_bits - 1, 0]
    parts = embed(n, series, emb_weight)
    got = hand_out(parts, "head")
    got[0] = call(bias_kernel, block)(parts[0], emb_bias.reshape(n, 1, width))
    cut = call(functools.partial(cut_kernel, bits), shape(heads_width >> len(bits), model))(out_weight)
    have = cut[None]
    for bit in bits_below(n):
        have = jnp.concatenate([have, send(have, "head", bit)], 0)
    rest = have[None, 1:]
    mine = call(add_kernel, block)(*got)
    emb = spread_out(mine, "head")
    for bit in bits:
        rest = jnp.concatenate([rest, send(rest, "var", 1 << bit)], 0)
    wide = halves_of(model, 2 * heads_width) + halves_of(model, heads_width)
    kv_hi, kv_lo, q_hi, q_lo = call(functools.partial(ordered_kernel, n), wide)(k_weight, v_weight, q_weight)
    pair = call(project_kernel, shape(rows, 2 * heads_width))(*emb, kv_hi, kv_lo)
    queries = call(project_kernel, shape(rows, heads_width))(*emb, q_hi, q_lo)
    first, later = gather_pieces(pair)
    ffn = call(split_kernel, halves_of(*ffn_in.shape) + halves_of(*ffn_out.shape))(ffn_in, ffn_out)
    order = functools.partial(order_kernel, bits)
    whole_out = call(order, halves_of(n * heads_width, model))(out_weight, rest)
    state = call(
        functools.partial(attend_kernel, merge=False), [shape(rows, heads_width)] * 3, limit=16
    )(queries, *first)
    mixed = call(
        functools.partial(attend_kernel, merge=True), shape(rows, heads_width), limit=16
    )(queries, *state, *later)
    mixes = spread_out(mixed, "head")
    partial = call(functools.partial(post_kernel, n), [block] * n, limit=16)(
        *mixes, *emb, *whole_out, norm1_gain[None, :], norm1_bias[None, :], *ffn
    )
    got = hand_out(partial, "head")
    flipped, stats = call(functools.partial(stats_kernel, n), [shape(width, rows), shape(2, rows)])(*got)
    return call(functools.partial(final_kernel, n), shape(width, rows))(
        flipped, *spread_out(stats, "head"), norm2_gain.reshape(n, 1, width), norm2_bias.reshape(n, 1, width)
    )


def solution(mesh):
    return jax.shard_map(
        on_device,
        mesh=mesh,
        in_specs=(
            P("var", "head"), P("head", None), P(), P(None, "head"), P(None, "head"), P(None, "head"),
            P("head", None), P(), P(), P(None, "head"), P("head", None), P(), P(),
        ),
        out_specs=P("head", "var"),
        check_vma=False,
    )
```

```python
import functools
import math

import jax
import jax.numpy as jnp
from jax import lax
from jax.experimental import pallas as pl
from jax.experimental.pallas import tpu as pltpu
from jax.sharding import PartitionSpec as P


DH = 64
EPS = 1e-05
F32 = jnp.float32
BF16 = jnp.bfloat16
MIB = 1 << 20


def split(x):
    hi = x.astype(BF16)
    return hi, (x - hi.astype(F32)).astype(BF16)


def mm(a, b, dims):
    return lax.dot_general(a, b, (dims, ((), ())), preferred_element_type=F32)


def dot3_split(a, b_hi, b_lo, dims=((1,), (0,))):
    a_hi, a_lo = split(a)
    rows = a.shape[0]
    first = mm(jnp.concatenate([a_hi, a_lo], 0), b_hi, dims)
    return first[:rows] + (first[rows:] + mm(a_hi, b_lo, dims))


def dot3(a, b, dims=((1,), (0,))):
    return dot3_split(a, *split(b), dims)


def butterfly(blocks, pos):
    count = len(blocks)
    out = list(blocks)
    bit = 1
    while bit < count:
        take = (pos & bit) != 0
        out = [jnp.where(take, out[j ^ bit], out[j]) for j in range(count)]
        bit *= 2
    return out


def columns(x, count):
    width = x.shape[1] // count
    return [x[:, j * width : (j + 1) * width] for j in range(count)]


def call(body, outs, scratch=(), limit=12, grid=None, in_specs=None, out_specs=None, flops=0, nbytes=0):
    kwargs = {}
    if grid is not None:
        kwargs = dict(grid=grid, in_specs=in_specs, out_specs=out_specs)
    return pl.pallas_call(
        body,
        out_shape=outs,
        scratch_shapes=list(scratch),
        compiler_params=pltpu.CompilerParams(vmem_limit_bytes=limit * MIB),
        cost_estimate=pl.CostEstimate(flops=flops, bytes_accessed=nbytes, transcendentals=0),
        **kwargs,
    )


def shape(*dims, dtype=F32):
    return jax.ShapeDtypeStruct(dims, dtype)


def halves_of(*dims):
    return [shape(*dims, dtype=BF16)] * 2


def embed_kernel(count, x_hbm, w_hbm, *rest):
    outs, (x_buf, w_buf, x_sems, w_sems) = rest[:count], rest[count:]
    pos = lax.axis_index("head")
    steps, step = w_buf.shape[0], w_buf.shape[1]
    halves, wide = x_buf.shape[0], x_buf.shape[2]
    x_copies = [
        pltpu.make_async_copy(x_hbm.at[:, pl.ds(at * wide, wide)], x_buf.at[at], x_sems.at[at]) for at in range(halves)
    ]
    w_copies = [
        pltpu.make_async_copy(w_hbm.at[pl.ds(at * step, step), :], w_buf.at[at], w_sems.at[at]) for at in range(steps)
    ]
    for at in range(steps):
        if (at * step) % wide == 0:
            x_copies[at * step // wide].start()
        w_copies[at].start()
    total = None
    for at in range(steps):
        half, start = divmod(at * step, wide)
        if start == 0:
            x_copies[half].wait()
        w_copies[at].wait()
        part = dot3(x_buf[half, :, start : start + step], w_buf[at])
        total = part if total is None else total + part
    for ref, block in zip(outs, butterfly(columns(total, count), pos)):
        ref[...] = block


def embed(count, series, emb_weight):
    rows, depth = series.shape
    model = emb_weight.shape[1]
    step = math.gcd(depth, 512)
    steps = depth // step
    halves = 2 if steps % 2 == 0 else 1
    hbm = pl.BlockSpec(memory_space=pltpu.HBM)
    return pl.pallas_call(
        functools.partial(embed_kernel, count),
        out_shape=[shape(rows, model // count)] * count,
        in_specs=[hbm, hbm],
        scratch_shapes=[
            pltpu.VMEM((halves, rows, depth // halves), F32),
            pltpu.VMEM((steps, step, model), F32),
            pltpu.SemaphoreType.DMA((halves,)),
            pltpu.SemaphoreType.DMA((steps,)),
        ],
        name="embed",
        compiler_params=pltpu.CompilerParams(vmem_limit_bytes=126 * MIB // 2),
        cost_estimate=pl.CostEstimate(
            flops=6 * rows * depth * model, bytes_accessed=4 * depth * (model + rows), transcendentals=0
        ),
    )(series, emb_weight)


def piece_of(index, bits):
    return sum(((index >> bit) & 1) << at for at, bit in enumerate(bits))


def cut_kernel(bits, w_ref, out):
    part = piece_of(lax.axis_index("var"), bits)
    size = out.shape[0]
    out[...] = w_ref[pl.ds(pl.multiple_of(part * size, size), size), :]


def order_kernel(bits, rest_ref, hi, lo):
    me = piece_of(lax.axis_index("var"), bits)
    pieces, others, size, _ = rest_ref.shape
    for apart in range(pieces):
        for k in range(others):
            at = pl.ds(pl.multiple_of(k * pieces * size + (me ^ apart) * size, size), size)
            hi[at, :], lo[at, :] = split(rest_ref[apart, k])


def bias_kernel(x_ref, bias, out):
    out[...] = x_ref[...] + bias[lax.axis_index("head")]


def add_kernel(*refs):
    total = refs[0][...]
    for part in refs[1:-1]:
        total = total + part[...]
    refs[-1][...] = total


def split_kernel(*refs):
    count = len(refs) // 3
    for at in range(count):
        refs[count + 2 * at][...], refs[count + 2 * at + 1][...] = split(refs[at][...])


def ordered_kernel(count, k_ref, v_ref, q_ref, *outs):
    pos = lax.axis_index("head")
    width, cols = k_ref.shape[0] // count, k_ref.shape[1]
    for k in range(count):
        rows = pl.ds(pl.multiple_of((pos ^ k) * width, width), width)
        at = slice(k * width, (k + 1) * width)
        outs[0][at, :cols], outs[1][at, :cols] = split(k_ref[rows, :])
        outs[0][at, cols:], outs[1][at, cols:] = split(v_ref[rows, :])
        outs[2][at, :], outs[3][at, :] = split(q_ref[rows, :] * (1.0 / math.sqrt(DH)))


def project_kernel(*refs):
    blocks, hi, lo, out = refs[:-3], *refs[-3:]
    out[...] = dot3_split(jnp.concatenate([block[...] for block in blocks], 1), hi[...], lo[...])


def by_head(stacked, heads):
    rows = stacked.shape[0] // heads
    lane = lax.broadcasted_iota(jnp.int32, (rows, stacked.shape[1]), 1) // DH
    out = stacked[:rows]
    for head in range(1, heads):
        out = jnp.where(lane == head, stacked[head * rows : (head + 1) * rows], out)
    return out


def attend_kernel(q_ref, *refs, merge):
    if merge:
        (acc_a, top_a, sum_a), pieces, out = refs[:3], refs[3:-1], refs[-1]
    else:
        pieces, (acc_out, top_out, sum_out) = refs[:-3], refs[-3:]
    rows, wide = q_ref.shape
    heads = wide // DH
    query = q_ref[...]
    lane = lax.broadcasted_iota(jnp.int32, query.shape, 1) // DH
    stacked = jnp.concatenate([jnp.where(lane == head, query, 0.0) for head in range(heads)], 0)
    k_hi, k_lo = split(jnp.concatenate([piece[:, :wide] for piece in pieces], 0))
    v_hi, v_lo = split(jnp.concatenate([piece[:, wide:] for piece in pieces], 0))
    s_hi, s_lo = split(stacked)
    queries = jnp.concatenate(
        [jnp.concatenate([s_hi, s_hi], 1), jnp.concatenate([s_lo, jnp.zeros_like(s_lo)], 1)], 0
    )
    scores = mm(queries, jnp.concatenate([k_hi, k_lo], 1), ((1,), (1,)))
    scores = scores[: heads * rows] + scores[heads * rows :]
    top = jnp.max(scores, axis=1, keepdims=True)
    weights = jnp.exp(scores - top)
    total = jnp.sum(weights, axis=1, keepdims=True)
    both = mm(jnp.concatenate(split(weights), 0), jnp.concatenate([v_hi, v_lo], 1), ((1,), (0,)))
    above, below = both[: heads * rows], both[heads * rows :]
    acc = by_head(above[:, :wide] + (above[:, wide:] + below[:, :wide]), heads)
    total = by_head(jnp.broadcast_to(total, (heads * rows, wide)), heads)
    top = by_head(jnp.broadcast_to(top, (heads * rows, wide)), heads)
    if merge:
        high = jnp.maximum(top, top_a[...])
        fade_a, fade = jnp.exp(top_a[...] - high), jnp.exp(top - high)
        out[...] = (acc * fade + acc_a[...] * fade_a) / (total * fade + sum_a[...] * fade_a)
    else:
        acc_out[...] = acc
        top_out[...] = top
        sum_out[...] = total


def normalise(x, gain, bias):
    centre = jnp.mean(x, axis=-1, keepdims=True)
    spread = x - centre
    variance = jnp.mean(spread * spread, axis=-1, keepdims=True)
    return spread * lax.rsqrt(variance + EPS) * gain + bias


def gelu(v):
    return 0.5 * v * (1.0 + lax.erf(v * (1.0 / math.sqrt(2.0))))


def own_kernel(mixed, weight, *refs):
    emb, out = refs[:-1], refs[-1]
    embedded = jnp.concatenate(butterfly([e[...] for e in emb], lax.axis_index("head")), 1)
    out[...] = embedded + dot3(mixed[...], weight[...])


def post_kernel(count, base, *refs):
    pos = lax.axis_index("head")
    mixed = refs[: count - 1]
    o_hi, o_lo, gain, bias, in_hi, in_lo, out_hi, out_lo = refs[count - 1 : count + 7]
    outs = refs[count + 7 :]
    stream = jnp.concatenate([m[...] for m in mixed], 1)
    attended = base[...] + dot3_split(stream, o_hi[...], o_lo[...])
    normed = normalise(attended, gain[...], bias[...])
    hidden = gelu(dot3_split(normed, in_hi[...], in_lo[...]))
    partial = butterfly(columns(dot3_split(hidden, out_hi[...], out_lo[...]), count), pos)
    mine = butterfly(columns(normed, count), pos)[0]
    outs[0][...] = mine + partial[0]
    for ref, block in zip(outs[1:], partial[1:]):
        ref[...] = block


def stats_kernel(count, *refs):
    parts, out, stats = refs[:count], refs[count], refs[count + 1]
    total = parts[0][...]
    for part in parts[1:]:
        total = total + part[...]
    flipped = total.T
    centre = jnp.mean(flipped, axis=0, keepdims=True)
    spread = flipped - centre
    out[...] = flipped
    stats[...] = jnp.concatenate([centre, jnp.sum(spread * spread, axis=0, keepdims=True)], 0)


def columns_kernel(gain, bias, *outs):
    pos = lax.axis_index("head")
    width, rows = outs[0].shape
    pair = jnp.concatenate([gain[pos], bias[pos], jnp.zeros((6, width), F32)], 0).T
    for at, out in enumerate(outs):
        out[...] = jnp.broadcast_to(pair[:, at : at + 1], (width, rows))


def final_kernel(count, x_ref, *refs):
    stats, (gain, bias, out) = refs[:count], refs[count:]
    width = x_ref.shape[0]
    centres = [s[0:1, :] for s in stats]
    centre = sum(centres[1:], centres[0]) * (1.0 / count)
    square = sum((s[1:2, :] for s in stats[1:]), stats[0][1:2, :])
    for each in centres:
        square = square + width * (each - centre) * (each - centre)
    scale = lax.rsqrt(square * (1.0 / (count * width)) + EPS)
    out[...] = (x_ref[...] - centre) * scale * gain[...] + bias[...]


def send(x, axis, offset):
    size = lax.axis_size(axis)
    return lax.ppermute(x, axis, [(i, i ^ offset) for i in range(size)])


def spread_out(x, axis):
    return [x] + [send(x, axis, k) for k in range(1, lax.axis_size(axis))]


def hand_out(parts, axis):
    return [parts[0]] + [send(parts[k], axis, k) for k in range(1, lax.axis_size(axis))]


def bits_below(count):
    return [1 << at for at in range(count.bit_length() - 1)]


def gather_pieces(piece):
    size = lax.axis_size("var")
    if size > 8:
        whole = lax.all_gather(piece, "var", axis=0, tiled=True)
        cut = whole.shape[0] // 2
        return [whole[:cut]], [whole[cut:]]
    far = [piece] + [send(piece, "var", k) for k in range(2, size, 2)]
    near = [send(each, "var", 1) for each in far]
    return far[:-1] + near[:-1], [far[-1], near[-1]]


def on_device(
    series, emb_weight, emb_bias, q_weight, k_weight, v_weight, out_weight,
    norm1_gain, norm1_bias, ffn_in, ffn_out, norm2_gain, norm2_bias,
):
    n = lax.axis_size("head")
    rows, _ = series.shape
    model = emb_weight.shape[1]
    width = model // n
    heads_width = q_weight.shape[1]
    block = shape(rows, width)

    var_bits = lax.axis_size("var").bit_length() - 1
    bits = [var_bits - 1, 0]
    parts = embed(n, series, emb_weight)
    got = hand_out(parts, "head")
    got[0] = call(bias_kernel, block)(parts[0], emb_bias.reshape(n, 1, width))
    cut = call(functools.partial(cut_kernel, bits), shape(heads_width >> len(bits), model))(out_weight)
    have = cut[None]
    for bit in bits_below(n):
        have = jnp.concatenate([have, send(have, "head", bit)], 0)
    rest = have[None, 1:]
    mine = call(add_kernel, block)(*got)
    emb = spread_out(mine, "head")
    for bit in bits:
        rest = jnp.concatenate([rest, send(rest, "var", 1 << bit)], 0)
    wide = halves_of(model, 2 * heads_width) + halves_of(model, heads_width)
    kv_hi, kv_lo, q_hi, q_lo = call(functools.partial(ordered_kernel, n), wide)(k_weight, v_weight, q_weight)
    pair = call(project_kernel, shape(rows, 2 * heads_width))(*emb, kv_hi, kv_lo)
    queries = call(project_kernel, shape(rows, heads_width))(*emb, q_hi, q_lo)
    first, later = gather_pieces(pair)
    ffn = call(split_kernel, halves_of(*ffn_in.shape) + halves_of(*ffn_out.shape))(ffn_in, ffn_out)
    order = functools.partial(order_kernel, bits)
    whole_out = call(order, halves_of((n - 1) * heads_width, model))(rest)
    state = call(
        functools.partial(attend_kernel, merge=False), [shape(rows, heads_width)] * 3, limit=16
    )(queries, *first)
    mixed = call(
        functools.partial(attend_kernel, merge=True), shape(rows, heads_width), limit=16
    )(queries, *state, *later)
    mixes = spread_out(mixed, "head")
    base = call(own_kernel, shape(rows, model))(mixed, out_weight, *emb)
    partial = call(functools.partial(post_kernel, n), [block] * n, limit=16)(
        base, *mixes[1:], *whole_out, norm1_gain[None, :], norm1_bias[None, :], *ffn
    )
    scales = call(columns_kernel, [shape(width, rows)] * 2)(
        norm2_gain.reshape(n, 1, width), norm2_bias.reshape(n, 1, width)
    )
    got = hand_out(partial, "head")
    flipped, stats = call(functools.partial(stats_kernel, n), [shape(width, rows), shape(2, rows)])(*got)
    return call(functools.partial(final_kernel, n), shape(width, rows))(flipped, *spread_out(stats, "head"), *scales)


def solution(mesh):
    return jax.shard_map(
        on_device,
        mesh=mesh,
        in_specs=(
            P("var", "head"), P("head", None), P(), P(None, "head"), P(None, "head"), P(None, "head"),
            P("head", None), P(), P(), P(None, "head"), P("head", None), P(), P(),
        ),
        out_specs=P("head", "var"),
        check_vma=False,
    )
```
